512 devices in a mesh: dp: 16 (over y, x), expert: 32 (over z, core).
Axes of the slice: x: 4, y: 4, z: 16, core: 2. Of those that a mesh axis runs over, the one named last changes fastest.
Arguments:
- tokens: bfloat16 [65536, 2048], P(('dp', 'expert')), may hold values from -6 to 6
- expert_ids: int32 [65536, 1], P(('dp', 'expert')), may hold values from 0 to 7; in each aligned block of 128 rows (0 to 127, 128 to 255, ...) at most 20 rows name the same one
- route_weight: float32 [65536, 1], P(('dp', 'expert')), may hold values from 0.1 to 1
- cotangent: bfloat16 [65536, 2048], P(('dp', 'expert')), may hold values from -0.59765625 to 0.59765625
- w_gate: bfloat16 [8192, 2048], P('expert', 'dp'), may hold values from -0.125 to 0.125
- w_up: bfloat16 [8192, 2048], P('expert', 'dp'), may hold values from -0.125 to 0.125
- w_down: bfloat16 [8192, 2048], P('expert', 'dp'), may hold values from -0.1875 to 0.1875
Outputs:
- layer_out: bfloat16 [65536, 2048], P(('dp', 'expert'))
- token_grad: bfloat16 [65536, 2048], P(('dp', 'expert'))
- gate_grad: bfloat16 [8192, 2048], P('expert', 'dp')
- up_grad: bfloat16 [8192, 2048], P('expert', 'dp')
- down_grad: bfloat16 [8192, 2048], P('expert', 'dp')
The draws below stay inside these ranges and needn't reach their ends.
Inputs may be any that keep to these rules, and one draw needn't show every extreme that they name: `expert_ids`: among the 128 rows of one device, at most 20 name the same expert.
All inputs are finite; a program needn't handle non-finite values.
Results may differ from the reference program's by a relative error of at most 0.018.
Values may be sent and summed in bfloat16 or wider, within the bound.
No kernel may reach another device: no remote copies, remote signals or barrier semaphores. Data moves between devices by JAX's collectives and lax.ppermute only.
A program may use at most 64 MiB of HBM per device.

```python
import math
import jax
import jax.numpy as jnp
import numpy as np
from jax import lax

D = 2048
H = 1024
EXPERTS = 8
TOK_DEV = 128
CAP = 20
GROUP = 4
HS = 256
TOKENS = 65536
N_DP = 16
N_EXPERT = 32


def block_levels(rng, shape, shards, smallest, largest):
    gain, own = 1.0, jax.random.fold_in(rng, 6)
    for dim, shards_of in shards:
        draws = jnp.exp(jax.random.uniform(jax.random.fold_in(own, dim), (shards_of,), jnp.float32, smallest / len(shards), largest / len(shards)))
        gain = gain * jnp.repeat(draws, shape[dim] // shards_of).reshape([-1 if axis == dim else 1 for axis in range(len(shape))])
    return gain


def routed_block(stream_key, own, number, rows, number_of, top, limit, skew):
    ranking = jax.random.permutation(stream_key, number_of)
    crowded, common = load_shares(number_of, rows * top, limit, skew, True), load_shares(number_of, rows * top, limit, skew, False)
    places = jnp.arange(number_of)

    def named(lengths, offset_by):
        used = int((lengths > 0).sum())
        fixed = max(1, used // 4)
        moved = fixed + (places - fixed + offset_by * (used - fixed)) % max(1, number_of - fixed)
        return jnp.zeros((number_of,), jnp.int32).at[ranking[jnp.where(places < fixed, places, moved)]].set(jnp.asarray(lengths, jnp.int32))

    lengths = jnp.where(number % 4 == 0, named(crowded, number // 4), named(common, number - number // 4 - 1))
    mixed = jax.random.permutation(jax.random.fold_in(own, 3), number_of)
    donor, receiver = mixed[0:number_of // 2 * 2:2], mixed[1:number_of // 2 * 2:2]
    slack = jnp.minimum(lengths[donor] - 1, limit - lengths[receiver]) // 2
    slack = jnp.where((donor == ranking[0]) | (receiver == ranking[0]) | (lengths[receiver] == 0), 0, jnp.maximum(slack, 0))
    moved = jax.random.randint(jax.random.fold_in(own, 4), (number_of // 2,), 0, 1 << 20) % (slack + 1)
    lengths = lengths.at[donor].add(-moved).at[receiver].add(moved)
    labels = jnp.searchsorted(jnp.cumsum(lengths), jnp.arange(rows * top), side="right").astype(jnp.int32)
    grid = labels.reshape(top, rows).T
    grid = grid[jax.random.permutation(jax.random.fold_in(own, 1), rows)]
    offset_by = jax.random.randint(jax.random.fold_in(own, 2), (rows, 1), 0, top)
    return jnp.take_along_axis(grid, (jnp.arange(top)[None, :] + offset_by) % top, axis=1)


def load_shares(count, total, limit, skew, full):
    weights = [(1 << 20) // math.isqrt(grade ** skew) + 1 for grade in range(1, count + 1)]
    largest = limit if full else min(limit, max(-(-total // count), total * weights[0] // sum(weights)))
    least = 1 if total - largest >= count - 1 else 0
    counts, surplus = [largest] + [least] * (count - 1), total - largest - least * (count - 1)
    while surplus > 0:
        movable = [i for i in range(1, count) if counts[i] < largest] or [i for i in range(1, count) if counts[i] < limit]
        whole, left = sum([weights[i] for i in movable]), surplus
        for i in movable:
            addition = min(limit - counts[i], max(1, left * weights[i] // whole), surplus)
            counts[i] = counts[i] + addition
            surplus = surplus - addition
    return np.array(counts)


def noise(key, dims, spread, most, split=(), held_as=jnp.bfloat16):
    values = spread * jax.random.normal(key, dims, jnp.float32)
    if split:
        values = values * block_levels(key, dims, split, -0.22, 0.18)
    return jnp.clip(values, -most, most).astype(held_as)


def setup_inputs(seed: int = 0) -> dict:
    arg_keys = jax.random.split(jax.random.key(seed), 8)
    tokens = noise(arg_keys[0], (TOKENS, D), 1.0, 6.0, ((0, 512),))
    expert_ids_keys = jax.random.split(jax.random.fold_in(arg_keys[1], 1), TOKENS // TOK_DEV)
    expert_ids_turns = jax.random.permutation(jax.random.fold_in(arg_keys[1], 3), TOKENS // TOK_DEV)
    expert_ids = jax.vmap(lambda own, number: routed_block(jax.random.fold_in(arg_keys[1], 2), own, number, TOK_DEV, EXPERTS, 1, CAP, 2))(expert_ids_keys, expert_ids_turns).reshape((TOKENS, 1))
    route_weight = jnp.clip(jnp.exp(math.log(1.0) - 2.3025851 * jax.random.uniform(arg_keys[2], (TOKENS, 1), jnp.float32) ** block_levels(arg_keys[2], (TOKENS, 1), ((0, 512),), -0.2, 0.2)), 0.1, 1.0)
    cotangent = noise(arg_keys[3], (TOKENS, D), 0.1, 0.59765625, ((0, 512),))
    w_gate = noise(arg_keys[4], (EXPERTS * H, D), D ** -0.5, 0.125, ((0, 32), (1, 16)))
    w_up = noise(arg_keys[5], (EXPERTS * H, D), D ** -0.5, 0.125, ((0, 32), (1, 16)))
    w_down = noise(arg_keys[6], (EXPERTS * H, D), H ** -0.5, 0.1875, ((0, 32), (1, 16)))
    return {"tokens": tokens, "expert_ids": expert_ids, "route_weight": route_weight, "cotangent": cotangent, "w_gate": w_gate, "w_up": w_up, "w_down": w_down}


def rounded_sum(partials):
    return jnp.sum(lax.optimization_barrier(partials.astype(jnp.bfloat16)).astype(jnp.float32), axis=0)


def reference(tokens, expert_ids, route_weight, cotangent, w_gate, w_up, w_down):
    features = tokens.shape[1]
    sources = N_EXPERT
    blocks = N_DP * N_EXPERT
    chosen = expert_ids[:, 0].reshape(blocks, TOK_DEV)
    onehot = (chosen[:, :, None] == jnp.arange(EXPERTS, dtype=jnp.int32)[None, None, :]).astype(jnp.int32)
    before = jnp.cumsum(onehot, axis=1) - onehot
    slot_index = (chosen * CAP + jnp.sum(before * onehot, axis=2)).astype(jnp.int32)
    slot_owner = jnp.full((blocks, EXPERTS * CAP), TOK_DEV, dtype=jnp.int32)
    block_ids = jnp.arange(blocks, dtype=jnp.int32)[:, None]
    token_ids = jnp.broadcast_to(jnp.arange(TOK_DEV, dtype=jnp.int32)[None, :], (blocks, TOK_DEV))
    slot_owner = slot_owner.at[block_ids, slot_index].set(token_ids)
    scaled = (route_weight * cotangent.astype(jnp.float32)).astype(jnp.bfloat16)
    source_ids = jnp.repeat(jnp.arange(sources, dtype=jnp.int32), CAP)
    zero_rows = jnp.zeros((sources * CAP, features), jnp.bfloat16)

    def one_expert(row_block, expert_pos):
        owners = lax.dynamic_slice(slot_owner, (row_block * sources, expert_pos * CAP), (sources, CAP)).reshape(-1)
        occupied = owners < TOK_DEV
        token_index = jnp.where(occupied, (row_block * sources + source_ids) * TOK_DEV + owners, 0).astype(jnp.int32)
        token_rows = jnp.where(occupied[:, None], tokens[token_index], zero_rows)
        grad_rows = jnp.where(occupied[:, None], scaled[token_index], zero_rows)
        weight_rows = jnp.where(occupied, route_weight[token_index, 0], jnp.zeros_like(route_weight[token_index, 0]))
        start = (expert_pos * H).astype(jnp.int32)
        gate_rows = lax.dynamic_slice_in_dim(w_gate, start, H, 0)
        up_rows = lax.dynamic_slice_in_dim(w_up, start, H, 0)
        down_rows = lax.dynamic_slice_in_dim(w_down, start, H, 0)
        gate_pre = jnp.dot(token_rows, gate_rows.T, preferred_element_type=jnp.float32)
        up_pre = jnp.dot(token_rows, up_rows.T, preferred_element_type=jnp.float32)
        gate_sigmoid = jax.nn.sigmoid(gate_pre)
        gate_silu = gate_pre * gate_sigmoid
        hidden = (gate_silu * up_pre).astype(jnp.bfloat16)
        count = hidden.shape[0]
        down_split = down_rows.astype(jnp.float32).reshape(GROUP, HS, features)
        gate_split = gate_rows.astype(jnp.float32).reshape(GROUP, HS, features)
        up_split = up_rows.astype(jnp.float32).reshape(GROUP, HS, features)
        out_terms = jnp.einsum("ngh,ghd->gnd", hidden.astype(jnp.float32).reshape(count, GROUP, HS), down_split)
        out_slots = (weight_rows[:, None] * rounded_sum(out_terms)).astype(jnp.bfloat16)
        hidden_grad = jnp.dot(grad_rows, down_rows.T, preferred_element_type=jnp.float32)
        gate_grad_pre = (hidden_grad * up_pre * (gate_sigmoid * (1.0 + gate_pre * (1.0 - gate_sigmoid)))).astype(jnp.bfloat16)
        up_grad_pre = (hidden_grad * gate_silu).astype(jnp.bfloat16)
        input_terms = jnp.einsum("ngh,ghd->gnd", gate_grad_pre.astype(jnp.float32).reshape(count, GROUP, HS), gate_split)
        input_terms = input_terms + jnp.einsum("ngh,ghd->gnd", up_grad_pre.astype(jnp.float32).reshape(count, GROUP, HS), up_split)
        back_slots = rounded_sum(input_terms).astype(jnp.bfloat16)
        gate_term = jnp.dot(gate_grad_pre.T, token_rows, preferred_element_type=jnp.float32).astype(jnp.bfloat16)
        up_term = jnp.dot(up_grad_pre.T, token_rows, preferred_element_type=jnp.float32).astype(jnp.bfloat16)
        down_term = jnp.dot(hidden.T, grad_rows, preferred_element_type=jnp.float32).astype(jnp.bfloat16)
        return out_slots, back_slots, gate_term, up_term, down_term

    def per_block(totals, row_block):
        results = lax.map(lambda expert_pos: one_expert(row_block, expert_pos), jnp.arange(EXPERTS, dtype=jnp.int32))
        out_slots, back_slots, gate_term, up_term, down_term = results
        gate_add = lax.optimization_barrier(gate_term).astype(jnp.float32).reshape(EXPERTS * H, features)
        up_add = lax.optimization_barrier(up_term).astype(jnp.float32).reshape(EXPERTS * H, features)
        down_add = lax.optimization_barrier(down_term).astype(jnp.float32).reshape(EXPERTS * H, features)
        return (totals[0] + gate_add, totals[1] + up_add, totals[2] + down_add), (out_slots, back_slots)

    zero_grads = jnp.zeros((EXPERTS * H, features), jnp.float32)
    totals, stacked = lax.scan(per_block, (zero_grads, zero_grads, zero_grads), jnp.arange(N_DP, dtype=jnp.int32))
    out_all, back_all = stacked
    slot_pos = slot_index - chosen * CAP
    flat = ((block_ids // sources) * EXPERTS + chosen) * (sources * CAP) + (block_ids % sources) * CAP + slot_pos
    flat = flat.reshape(-1).astype(jnp.int32)
    layer_out = out_all.reshape(-1, features)[flat]
    token_grad = back_all.reshape(-1, features)[flat]
    return (layer_out, token_grad, totals[0].astype(jnp.bfloat16), totals[1].astype(jnp.bfloat16), totals[2].astype(jnp.bfloat16))
```

```python
import jax
import jax.numpy as jnp
from jax import lax
from jax.experimental import pallas as pl
from jax.experimental.pallas import tpu as pltpu
from jax.sharding import Mesh
from jax.sharding import PartitionSpec as P

BF16 = jnp.bfloat16
F32 = jnp.float32

D = 2048
HS = 256
TOK = 128
FULL = 16
QUART = D // 4
MSG = D + QUART
ROWS = 8 * FULL
TAIL = 32
HALF = 2 * (ROWS + TAIL)

ALL = ("y", "x", "pair", "side", "core")
DP = ("y", "x")
EXPERT = ("pair", "side", "core")
SWAP = [(0, 1), (1, 0)]

VMEM_LIMIT = 48 * 2**20


def _iota(shape, dim):
    return lax.broadcasted_iota(jnp.int32, shape, dim)


def _dot(a, b):
    return lax.dot_general(a, b, (((1,), (0,)), ((), ())), preferred_element_type=F32)


def _dot_nt(a, b):
    return lax.dot_general(a, b, (((1,), (1,)), ((), ())), preferred_element_type=F32)


def _dot_tn(a, b):
    return lax.dot_general(a, b, (((0,), (0,)), ((), ())), preferred_element_type=F32)


def _placing(ids):
    onehot = (ids == _iota((16, TOK), 0)).astype(F32)
    earlier = (_iota((TOK, TOK), 0) < _iota((TOK, TOK), 1)).astype(F32).astype(BF16)
    before = _dot(onehot.astype(BF16), earlier)
    rank = jnp.sum(before * onehot, axis=0, keepdims=True).astype(jnp.int32)
    row = _iota((ROWS, TOK), 0)
    whole = row == jnp.where(rank < FULL, ids * FULL + rank, -1)
    first = jnp.where(rank < FULL, -8, ids * FULL + (rank - FULL) * 4)
    quarters = [row == first + c for c in range(4)]
    return whole, quarters


def _row_weights(mask, weight):
    return jnp.sum(jnp.where(mask, weight, 0.0), axis=1, keepdims=True)


def _send_kernel(ids_ref, weight_ref, tokens_ref, cot_ref, out_ref):
    whole, quarters = _placing(ids_ref[...])
    weight = weight_ref[...]
    whole_w = _row_weights(whole, weight)
    quarter_w = sum(_row_weights(q, weight) for q in quarters)
    whole_m = whole.astype(F32).astype(BF16)
    quarter_m = [q.astype(F32).astype(BF16) for q in quarters]
    for at, ref in ((0, tokens_ref), (MSG, cot_ref)):
        tail = jnp.zeros((ROWS, QUART), F32)
        for c in range(4):
            part = ref[:, c * QUART : (c + 1) * QUART]
            main = _dot(whole_m, part)
            if at:
                main = main * whole_w
            out_ref[:, at + c * QUART : at + (c + 1) * QUART] = main.astype(BF16)
            tail = tail + _dot(quarter_m[c], part)
        if at:
            tail = tail * quarter_w
        out_ref[:, at + D : at + MSG] = tail.astype(BF16)


def _send(ids, weight, tokens, cotangent):
    return pl.pallas_call(
        _send_kernel,
        out_shape=jax.ShapeDtypeStruct((ROWS, 2 * MSG), BF16),
        compiler_params=pltpu.CompilerParams(vmem_limit_bytes=VMEM_LIMIT),
        cost_estimate=pl.CostEstimate(flops=2**28, bytes_accessed=5 * 2**19, transcendentals=0),
        name="send",
    )(ids, weight, tokens, cotangent)


def _take_kernel(ids_ref, weight_ref, back_ref, out_ref, grad_ref):
    whole, quarters = _placing(ids_ref[...])
    weight = weight_ref[...]
    whole_w = _row_weights(whole, weight)
    quarter_w = sum(_row_weights(q, weight) for q in quarters)
    whole_m = whole.astype(F32).T.astype(BF16)
    quarter_m = [q.astype(F32).T.astype(BF16) for q in quarters]
    for at, ref in ((0, out_ref), (MSG, grad_ref)):
        tail = back_ref[:, at + D : at + MSG]
        if not at:
            tail = (tail.astype(F32) * quarter_w).astype(BF16)
        for c in range(4):
            main = back_ref[:, at + c * QUART : at + (c + 1) * QUART]
            if not at:
                main = (main.astype(F32) * whole_w).astype(BF16)
            both = _dot(whole_m, main) + _dot(quarter_m[c], tail)
            ref[:, c * QUART : (c + 1) * QUART] = both.astype(BF16)


def _take(ids, weight, back):
    return pl.pallas_call(
        _take_kernel,
        out_shape=[jax.ShapeDtypeStruct((TOK, D), BF16)] * 2,
        compiler_params=pltpu.CompilerParams(vmem_limit_bytes=VMEM_LIMIT),
        cost_estimate=pl.CostEstimate(flops=2**28, bytes_accessed=5 * 2**19, transcendentals=0),
        name="take",
    )(ids, weight, back)


def _tail_row(shape, row_dim, c):
    slot, row = _iota(shape, 1 - row_dim), _iota(shape, row_dim)
    mask = row == (slot // 4) * FULL + (slot % 4) * 4 + c
    return mask.astype(F32).astype(BF16)


def _expert_kernel(a_ref, b_ref, w_ref, oa_ref, ob_ref, h_ref, xt_ref, xg_ref):
    for i, ref in enumerate((a_ref, b_ref)):
        for at, x_ref in ((0, xt_ref), (MSG, xg_ref)):
            x_ref[i * ROWS : (i + 1) * ROWS, :] = ref[:, at : at + D]
            tail = ref[:, at + D : at + MSG]
            for c in range(4):
                x_ref[2 * ROWS + i * TAIL : 2 * ROWS + (i + 1) * TAIL, c * QUART : (c + 1) * QUART] = (
                    _dot(_tail_row((TAIL, ROWS), 1, c), tail).astype(BF16)
                )
    gate_up = _dot_nt(xt_ref[...], w_ref[: 2 * HS, :])
    hidden_grad = _dot_nt(xg_ref[...], w_ref[2 * HS :, :])
    gate, up = gate_up[:, :HS], gate_up[:, HS:]
    sig = jax.nn.sigmoid(gate)
    silu = gate * sig
    hidden = (silu * up).astype(BF16)
    h_ref[:, :HS] = (hidden_grad * up * (sig * (1.0 + gate * (1.0 - sig)))).astype(BF16)
    h_ref[:, HS : 2 * HS] = (hidden_grad * silu).astype(BF16)
    h_ref[:, 2 * HS :] = hidden
    for at, h_cols, w_rows in (
        (0, slice(2 * HS, 3 * HS), slice(2 * HS, 3 * HS)),
        (MSG, slice(0, 2 * HS), slice(0, 2 * HS)),
    ):
        tails = [jnp.zeros((ROWS, QUART), F32), jnp.zeros((ROWS, QUART), F32)]
        for c in range(4):
            cols = slice(c * QUART, (c + 1) * QUART)
            y = _dot(h_ref[:, h_cols], w_ref[w_rows, cols]).astype(BF16)
            for i, ref in enumerate((oa_ref, ob_ref)):
                ref[:, at + c * QUART : at + (c + 1) * QUART] = y[i * ROWS : (i + 1) * ROWS]
                tail = y[2 * ROWS + i * TAIL : 2 * ROWS + (i + 1) * TAIL]
                tails[i] = tails[i] + _dot(_tail_row((ROWS, TAIL), 0, c), tail)
        for i, ref in enumerate((oa_ref, ob_ref)):
            ref[:, at + D : at + MSG] = tails[i].astype(BF16)


def _expert(a, b, weights):
    return pl.pallas_call(
        _expert_kernel,
        out_shape=[jax.ShapeDtypeStruct((ROWS, 2 * MSG), BF16)] * 2
        + [jax.ShapeDtypeStruct((HALF, 3 * HS), BF16)]
        + [jax.ShapeDtypeStruct((HALF, D), BF16)] * 2,
        compiler_params=pltpu.CompilerParams(vmem_limit_bytes=VMEM_LIMIT),
        cost_estimate=pl.CostEstimate(
            flops=12 * HALF * HS * D, bytes_accessed=12 * 2**20, transcendentals=HALF * HS
        ),
        name="expert",
    )(a, b, weights)


def _terms_kernel(ha_ref, hb_ref, ta_ref, tb_ref, ga_ref, gb_ref, out_ref):
    gu = _dot_tn(ha_ref[:, : 2 * HS], ta_ref[...]) + _dot_tn(hb_ref[:, : 2 * HS], tb_ref[...])
    dn = _dot_tn(ha_ref[:, 2 * HS :], ga_ref[...]) + _dot_tn(hb_ref[:, 2 * HS :], gb_ref[...])
    for i in range(QUART // 128):
        cols = slice(i * 128, (i + 1) * 128)
        out_ref[i, : 2 * HS, :] = gu[:, cols].astype(BF16)
        out_ref[i, 2 * HS :, :] = dn[:, cols].astype(BF16)


def _terms(ha, hb, ta, tb, ga, gb):
    h_spec = pl.BlockSpec((HALF, 3 * HS), lambda i: (0, 0))
    x_spec = pl.BlockSpec((HALF, QUART), lambda i: (0, i))
    return pl.pallas_call(
        _terms_kernel,
        grid=(4,),
        in_specs=[h_spec] * 2 + [x_spec] * 4,
        out_specs=pl.BlockSpec((QUART // 128, 3 * HS, 128), lambda i: (i, 0, 0)),
        out_shape=jax.ShapeDtypeStruct((D // 128, 3 * HS, 128), BF16),
        compiler_params=pltpu.CompilerParams(vmem_limit_bytes=VMEM_LIMIT),
        cost_estimate=pl.CostEstimate(
            flops=12 * HALF * HS * D, bytes_accessed=10 * 2**20, transcendentals=0
        ),
        name="terms",
    )(ha, hb, ta, tb, ga, gb)


def _exchange(x):
    return lax.all_to_all(
        x.reshape(8, FULL, 2 * MSG), "pair", split_axis=0, concat_axis=0, tiled=True
    ).reshape(ROWS, 2 * MSG)


def _add(a, b):
    return (a.astype(F32) + b.astype(F32)).astype(BF16)


def local(tokens, expert_ids, route_weight, cotangent, w_gate, w_up, w_down):
    ids = expert_ids.reshape(1, TOK)
    weight = route_weight.reshape(1, TOK)
    weights = lax.all_gather(
        jnp.concatenate([w_gate, w_up, w_down], axis=0), DP, axis=1, tiled=True
    )
    own = _exchange(_send(ids, weight, tokens, cotangent))
    from_side = lax.ppermute(own, "side", SWAP)
    from_core = lax.ppermute(own, "core", SWAP)
    out_own, out_core, ha, ta, ga = _expert(own, from_core, weights)
    from_both = lax.ppermute(from_side, "core", SWAP)
    out_side, out_both, hb, tb, gb = _expert(from_side, from_both, weights)
    side_sum = _add(out_side, lax.ppermute(out_both, "core", SWAP))
    own_sum = out_own.astype(F32) + lax.ppermute(out_core, "core", SWAP).astype(F32)
    total = (own_sum + lax.ppermute(side_sum, "side", SWAP).astype(F32)).astype(BF16)
    terms = _terms(ha, hb, ta, tb, ga, gb).reshape(D // 128 * 3 * HS, 128)
    grads = lax.psum_scatter(terms, DP, scatter_dimension=0, tiled=True)
    layer_out, token_grad = _take(ids, weight, _exchange(total))
    return layer_out, token_grad, grads[:HS], grads[HS : 2 * HS], grads[2 * HS :]


def solution(mesh):
    fine = Mesh(mesh.devices.reshape(4, 4, 8, 2, 2), ALL)
    return jax.shard_map(
        local,
        mesh=fine,
        in_specs=(P(ALL, None),) * 4 + (P(EXPERT, DP),) * 3,
        out_specs=(P(ALL, None),) * 2 + (P(EXPERT, DP),) * 3,
        check_vma=False,
    )
```

```python
import jax
import jax.numpy as jnp
from jax import lax
from jax.experimental import pallas as pl
from jax.experimental.pallas import tpu as pltpu
from jax.sharding import Mesh
from jax.sharding import PartitionSpec as P

BF16 = jnp.bfloat16
F32 = jnp.float32

D = 2048
HS = 256
TOK = 128
FULL = 16
QUART = D // 4
MSG = D + QUART
ROWS = 8 * FULL
TAIL = 32
SLOTS = 2 * (ROWS + TAIL)

ALL = ("y", "x", "pair", "side", "core")
DP = ("y", "x")
EXPERT = ("pair", "side", "core")
SWAP = [(0, 1), (1, 0)]

VMEM_LIMIT = 48 * 2**20


def _iota(shape, dim):
    return lax.broadcasted_iota(jnp.int32, shape, dim)


def _dot(a, b):
    return lax.dot_general(a, b, (((1,), (0,)), ((), ())), preferred_element_type=F32)


def _dot_nt(a, b):
    return lax.dot_general(a, b, (((1,), (1,)), ((), ())), preferred_element_type=F32)


def _dot_tn(a, b):
    return lax.dot_general(a, b, (((0,), (0,)), ((), ())), preferred_element_type=F32)


def _placing(ids):
    onehot = (ids == _iota((16, TOK), 0)).astype(F32)
    earlier = (_iota((TOK, TOK), 0) < _iota((TOK, TOK), 1)).astype(F32).astype(BF16)
    before = _dot(onehot.astype(BF16), earlier)
    rank = jnp.sum(before * onehot, axis=0, keepdims=True).astype(jnp.int32)
    row = _iota((ROWS, TOK), 0)
    whole = row == jnp.where(rank < FULL, ids * FULL + rank, -1)
    first = jnp.where(rank < FULL, -8, ids * FULL + (rank - FULL) * 4)
    quarters = [row == first + c for c in range(4)]
    return whole, quarters


def _row_weights(mask, weight):
    return jnp.sum(jnp.where(mask, weight, 0.0), axis=1, keepdims=True)


def _send_kernel(ids_ref, weight_ref, tokens_hbm, cot_hbm, out_ref, tokens_ref, cot_ref, sems):
    copies = [
        pltpu.make_async_copy(tokens_hbm, tokens_ref, sems.at[0]),
        pltpu.make_async_copy(cot_hbm, cot_ref, sems.at[1]),
    ]
    for copy in copies:
        copy.start()
    whole, quarters = _placing(ids_ref[...])
    weight = weight_ref[...]
    whole_w = _row_weights(whole, weight)
    quarter_w = sum(_row_weights(q, weight) for q in quarters)
    whole_m = whole.astype(F32).astype(BF16)
    quarter_m = [q.astype(F32).astype(BF16) for q in quarters]
    for at, ref, copy in ((0, tokens_ref, copies[0]), (MSG, cot_ref, copies[1])):
        copy.wait()
        tail = jnp.zeros((ROWS, QUART), F32)
        for c in range(4):
            part = ref[:, c * QUART : (c + 1) * QUART]
            main = _dot(whole_m, part)
            if at:
                main = main * whole_w
            out_ref[:, at + c * QUART : at + (c + 1) * QUART] = main.astype(BF16)
            tail = tail + _dot(quarter_m[c], part)
        if at:
            tail = tail * quarter_w
        out_ref[:, at + D : at + MSG] = tail.astype(BF16)


def _send(ids, weight, tokens, cotangent):
    return pl.pallas_call(
        _send_kernel,
        in_specs=[pl.BlockSpec(memory_space=pltpu.VMEM)] * 2
        + [pl.BlockSpec(memory_space=pl.ANY)] * 2,
        out_shape=jax.ShapeDtypeStruct((ROWS, 2 * MSG), BF16),
        scratch_shapes=[pltpu.VMEM((TOK, D), BF16)] * 2 + [pltpu.SemaphoreType.DMA((2,))],
        compiler_params=pltpu.CompilerParams(vmem_limit_bytes=VMEM_LIMIT),
        cost_estimate=pl.CostEstimate(flops=2**28, bytes_accessed=5 * 2**19, transcendentals=0),
        name="send",
    )(ids, weight, tokens, cotangent)


def _take_kernel(ids_ref, weight_ref, back_ref, out_ref, grad_ref):
    whole, quarters = _placing(ids_ref[...])
    weight = weight_ref[...]
    whole_w = _row_weights(whole, weight)
    quarter_w = sum(_row_weights(q, weight) for q in quarters)
    whole_m = whole.astype(F32).T.astype(BF16)
    quarter_m = [q.astype(F32).T.astype(BF16) for q in quarters]
    for at, ref in ((0, out_ref), (MSG, grad_ref)):
        tail = back_ref[:, at + D : at + MSG]
        if not at:
            tail = (tail.astype(F32) * quarter_w).astype(BF16)
        for c in range(4):
            main = back_ref[:, at + c * QUART : at + (c + 1) * QUART]
            if not at:
                main = (main.astype(F32) * whole_w).astype(BF16)
            both = _dot(whole_m, main) + _dot(quarter_m[c], tail)
            ref[:, c * QUART : (c + 1) * QUART] = both.astype(BF16)


def _take(ids, weight, back):
    return pl.pallas_call(
        _take_kernel,
        out_shape=[jax.ShapeDtypeStruct((TOK, D), BF16)] * 2,
        compiler_params=pltpu.CompilerParams(vmem_limit_bytes=VMEM_LIMIT),
        cost_estimate=pl.CostEstimate(flops=2**28, bytes_accessed=5 * 2**19, transcendentals=0),
        name="take",
    )(ids, weight, back)


def _tail_row(shape, row_dim, c):
    slot, row = _iota(shape, 1 - row_dim), _iota(shape, row_dim)
    mask = row == (slot // 4) * FULL + (slot % 4) * 4 + c
    return mask.astype(F32).astype(BF16)


def _column(ref, block, rows):
    return ref.at[rows, pl.ds(pl.multiple_of(block * 128, 128), 128)]


def _expert_kernel(pos_ref, a_ref, b_ref, *refs):
    pieces, (oa_ref, ob_ref, h_ref, xt_ref, xg_ref, w_ref, sems) = refs[:8], refs[8:]
    y, x = pos_ref[0], pos_ref[1]
    copies = []
    for half in range(2):
        for outer in range(4):
            for inner in range(4):
                dy, dx = (inner, outer) if half == 0 else (outer, inner)
                block = lax.rem(y + 4 - dy, 4) * 4 + lax.rem(x + 4 - dx, 4)
                copy = pltpu.make_async_copy(
                    pieces[half * 4 + outer].at[inner],
                    _column(w_ref, block, pl.ds(half * 3 * HS, 3 * HS)),
                    sems.at[len(copies)],
                )
                copy.start()
                copies.append(copy)
    for i, ref in enumerate((a_ref, b_ref)):
        for at, x_ref in ((0, xt_ref), (MSG, xg_ref)):
            x_ref[i * ROWS : (i + 1) * ROWS, :] = ref[:, at : at + D]
            tail = ref[:, at + D : at + MSG]
            for c in range(4):
                x_ref[2 * ROWS + i * TAIL : 2 * ROWS + (i + 1) * TAIL, c * QUART : (c + 1) * QUART] = (
                    _dot(_tail_row((TAIL, ROWS), 1, c), tail).astype(BF16)
                )
    for half in range(2):
        for copy in copies[half * 16 : half * 16 + 16]:
            copy.wait()
        base = half * 3 * HS
        gate_up = _dot_nt(xt_ref[...], w_ref[base : base + 2 * HS, :])
        hidden_grad = _dot_nt(xg_ref[...], w_ref[base + 2 * HS : base + 3 * HS, :])
        gate, up = gate_up[:, :HS], gate_up[:, HS:]
        sig = jax.nn.sigmoid(gate)
        silu = gate * sig
        h_ref[:, base : base + HS] = (
            hidden_grad * up * (sig * (1.0 + gate * (1.0 - sig)))
        ).astype(BF16)
        h_ref[:, base + HS : base + 2 * HS] = (hidden_grad * silu).astype(BF16)
        h_ref[:, base + 2 * HS : base + 3 * HS] = (silu * up).astype(BF16)
    for at, first, last in ((0, 2 * HS, 3 * HS), (MSG, 0, 2 * HS)):
        own, side = slice(first, last), slice(3 * HS + first, 3 * HS + last)
        tails = [jnp.zeros((ROWS, QUART), F32), jnp.zeros((ROWS, QUART), F32)]
        for c in range(4):
            cols = slice(c * QUART, (c + 1) * QUART)
            y = _dot(h_ref[:, own], w_ref[own, cols]) + _dot(h_ref[:, side], w_ref[side, cols])
            y = y.astype(BF16)
            for i, ref in enumerate((oa_ref, ob_ref)):
                ref[:, at + c * QUART : at + (c + 1) * QUART] = y[i * ROWS : (i + 1) * ROWS]
                tail = y[2 * ROWS + i * TAIL : 2 * ROWS + (i + 1) * TAIL]
                tails[i] = tails[i] + _dot(_tail_row((ROWS, TAIL), 0, c), tail)
        for i, ref in enumerate((oa_ref, ob_ref)):
            ref[:, at + D : at + MSG] = tails[i].astype(BF16)


def _expert(pos, a, b, pieces):
    vmem = pl.BlockSpec(memory_space=pltpu.VMEM)
    return pl.pallas_call(
        _expert_kernel,
        in_specs=[pl.BlockSpec(memory_space=pltpu.SMEM)] + [vmem] * 2
        + [pl.BlockSpec(memory_space=pl.ANY)] * 8,
        out_specs=[vmem] * 5,
        out_shape=[jax.ShapeDtypeStruct((ROWS, 2 * MSG), BF16)] * 2
        + [jax.ShapeDtypeStruct((SLOTS, 6 * HS), BF16)]
        + [jax.ShapeDtypeStruct((SLOTS, D), BF16)] * 2,
        scratch_shapes=[pltpu.VMEM((6 * HS, D), BF16), pltpu.SemaphoreType.DMA((32,))],
        compiler_params=pltpu.CompilerParams(vmem_limit_bytes=VMEM_LIMIT),
        cost_estimate=pl.CostEstimate(
            flops=24 * SLOTS * HS * D, bytes_accessed=16 * 2**20, transcendentals=2 * SLOTS * HS
        ),
        name="expert",
    )(pos, a, b, *pieces)


def _terms_kernel(pos_ref, h_ref, t_ref, g_ref, *refs):
    outs, (held, sems) = refs[:8], refs[8:]
    row = pl.program_id(0)
    dy = lax.rem(row - pos_ref[0] + 4, 4)
    for half in range(2):
        base = half * 3 * HS
        gate_up = _dot_tn(h_ref[:, base : base + 2 * HS], t_ref[...]).astype(BF16)
        down = _dot_tn(h_ref[:, base + 2 * HS : base + 3 * HS], g_ref[...]).astype(BF16)
        for col in range(4):
            cols = slice(col * 128, (col + 1) * 128)
            held[row * 8 + half * 4 + col, : 2 * HS, :] = gate_up[:, cols]
            held[row * 8 + half * 4 + col, 2 * HS :, :] = down[:, cols]
            dx = lax.rem(col - pos_ref[1] + 4, 4)
            outer, inner = (dx, dy) if half == 0 else (dy, dx)
            slot = row * 8 + half * 4 + col
            for d in range(4):

                @pl.when(outer == d)
                def _(out=outs[half * 4 + d], slot=slot, inner=inner):
                    pltpu.make_async_copy(held.at[slot], out.at[inner], sems.at[slot]).start()

    @pl.when(row == 3)
    def _():
        for slot in range(32):
            pltpu.make_async_copy(held.at[slot], outs[0].at[0], sems.at[slot]).wait()


def _terms(pos, h, t, g):
    x_spec = pl.BlockSpec((SLOTS, QUART), lambda i: (0, i))
    return pl.pallas_call(
        _terms_kernel,
        grid=(4,),
        in_specs=[
            pl.BlockSpec(memory_space=pltpu.SMEM),
            pl.BlockSpec((SLOTS, 6 * HS), lambda i: (0, 0)),
            x_spec,
            x_spec,
        ],
        out_specs=[pl.BlockSpec(memory_space=pl.ANY)] * 8,
        out_shape=[jax.ShapeDtypeStruct((4, 3 * HS, 128), BF16)] * 8,
        scratch_shapes=[pltpu.VMEM((32, 3 * HS, 128), BF16), pltpu.SemaphoreType.DMA((32,))],
        compiler_params=pltpu.CompilerParams(vmem_limit_bytes=VMEM_LIMIT),
        cost_estimate=pl.CostEstimate(
            flops=12 * SLOTS * HS * D, bytes_accessed=10 * 2**20, transcendentals=0
        ),
        name="terms",
    )(pos, h, t, g)


def _shift(x, axis, d):
    return lax.ppermute(x, axis, [(i, (i + d) % 4) for i in range(4)])


def _gather_pieces(piece, first, second):
    stack = jnp.stack([piece] + [_shift(piece, first, d) for d in (1, 2, 3)])
    return [stack] + [_shift(stack, second, d) for d in (1, 2, 3)]


def _sum(parts):
    return sum(p.astype(F32) for p in parts)


def _scatter_terms(parts, first, second):
    half = _sum([parts[0]] + [_shift(parts[d], first, d) for d in (2, 1, 3)]).astype(BF16)
    return _sum([half[0]] + [_shift(half[d], second, d) for d in (2, 1, 3)])


def _exchange(x):
    return lax.all_to_all(
        x.reshape(8, FULL, 2 * MSG), "pair", split_axis=0, concat_axis=0, tiled=True
    ).reshape(ROWS, 2 * MSG)


def _add(a, b):
    return (a.astype(F32) + b.astype(F32)).astype(BF16)


def local(tokens, expert_ids, route_weight, cotangent, w_gate, w_up, w_down):
    ids = expert_ids.reshape(1, TOK)
    weight = route_weight.reshape(1, TOK)
    pos = jnp.stack([lax.axis_index("y"), lax.axis_index("x")]).astype(jnp.int32)
    sent = _send(ids, weight, tokens, cotangent)
    own_piece = jnp.concatenate([w_gate, w_up, w_down], axis=0)
    side_piece = lax.ppermute(own_piece, "side", SWAP)
    pieces = _gather_pieces(own_piece, "y", "x") + _gather_pieces(side_piece, "x", "y")
    own = _exchange(sent)
    from_core = lax.ppermute(own, "core", SWAP)
    out_own, out_core, h, t, g = _expert(pos, own, from_core, pieces)
    total = _add(out_own, lax.ppermute(out_core, "core", SWAP))
    terms = _terms(pos, h, t, g)
    own_terms = _scatter_terms(terms[:4], "x", "y")
    side_terms = _scatter_terms(terms[4:], "y", "x").astype(BF16)
    grads = (own_terms + lax.ppermute(side_terms, "side", SWAP).astype(F32)).astype(BF16)
    layer_out, token_grad = _take(ids, weight, _exchange(total))
    return layer_out, token_grad, grads[:HS], grads[HS : 2 * HS], grads[2 * HS :]


def solution(mesh):
    fine = Mesh(mesh.devices.reshape(4, 4, 8, 2, 2), ALL)
    return jax.shard_map(
        local,
        mesh=fine,
        in_specs=(P(ALL, None),) * 4 + (P(EXPERT, DP),) * 3,
        out_specs=(P(ALL, None),) * 2 + (P(EXPERT, DP),) * 3,
        check_vma=False,
    )
```

```python
import jax
import jax.numpy as jnp
from jax import lax
from jax.experimental import pallas as pl
from jax.experimental.pallas import tpu as pltpu
from jax.sharding import Mesh
from jax.sharding import PartitionSpec as P

BF16 = jnp.bfloat16
F32 = jnp.float32

D = 2048
HS = 256
TOK = 128
FULL = 16
QUART = D // 4
MSG = D + QUART
ROWS = 8 * FULL
TAIL = 32
SLOTS = 2 * (ROWS + TAIL)

ALL = ("y", "x", "pair", "side", "core")
DP = ("y", "x")
EXPERT = ("pair", "side", "core")
SWAP = [(0, 1), (1, 0)]

VMEM_LIMIT = 60 * 2**20


def _iota(shape, dim):
    return lax.broadcasted_iota(jnp.int32, shape, dim)


def _dot(a, b):
    return lax.dot_general(a, b, (((1,), (0,)), ((), ())), preferred_element_type=F32)


def _dot_nt(a, b):
    return lax.dot_general(a, b, (((1,), (1,)), ((), ())), preferred_element_type=F32)


def _dot_tn(a, b):
    return lax.dot_general(a, b, (((0,), (0,)), ((), ())), preferred_element_type=F32)


def _placing(ids):
    onehot = (ids == _iota((16, TOK), 0)).astype(F32)
    earlier = (_iota((TOK, TOK), 0) < _iota((TOK, TOK), 1)).astype(F32).astype(BF16)
    before = _dot(onehot.astype(BF16), earlier)
    rank = jnp.sum(before * onehot, axis=0, keepdims=True).astype(jnp.int32)
    row = _iota((ROWS, TOK), 0)
    whole = row == jnp.where(rank < FULL, ids * FULL + rank, -1)
    first = jnp.where(rank < FULL, -8, ids * FULL + (rank - FULL) * 4)
    quarters = [row == first + c for c in range(4)]
    return whole, quarters


def _row_weights(mask, weight):
    return jnp.sum(jnp.where(mask, weight, 0.0), axis=1, keepdims=True)


def _pack_kernel(gate_ref, up_ref, down_ref, out_ref, sems):
    copies = [
        pltpu.make_async_copy(ref, out_ref.at[pl.ds(i * HS, HS), :], sems.at[i])
        for i, ref in enumerate((gate_ref, up_ref, down_ref))
    ]
    for copy in copies:
        copy.start()
    for copy in copies:
        copy.wait()


def _pack(gate, up, down):
    return pl.pallas_call(
        _pack_kernel,
        in_specs=[pl.BlockSpec(memory_space=pltpu.HBM)] * 3,
        out_specs=pl.BlockSpec(memory_space=pltpu.HBM),
        out_shape=jax.ShapeDtypeStruct((3 * HS, 128), BF16),
        scratch_shapes=[pltpu.SemaphoreType.DMA((3,))],
        compiler_params=pltpu.CompilerParams(vmem_limit_bytes=VMEM_LIMIT),
        cost_estimate=pl.CostEstimate(flops=0, bytes_accessed=3 * 2**17, transcendentals=0),
        name="pack",
    )(gate, up, down)


def _send_kernel(*refs):
    hbm, out_ref, held, sems = refs[:4], refs[4], refs[5:9], refs[9]
    ids_ref, weight_ref, tokens_ref, cot_ref = held
    copies = [pltpu.make_async_copy(hbm[i], held[i], sems.at[i]) for i in range(4)]
    for copy in copies:
        copy.start()
    copies[0].wait()
    copies[1].wait()
    whole, quarters = _placing(ids_ref[...])
    weight = weight_ref[...]
    whole_w = _row_weights(whole, weight)
    quarter_w = sum(_row_weights(q, weight) for q in quarters)
    whole_m = whole.astype(F32).astype(BF16)
    quarter_m = [q.astype(F32).astype(BF16) for q in quarters]
    for at, ref, copy in ((0, tokens_ref, copies[2]), (MSG, cot_ref, copies[3])):
        copy.wait()
        tail = jnp.zeros((ROWS, QUART), F32)
        for c in range(4):
            part = ref[:, c * QUART : (c + 1) * QUART]
            main = _dot(whole_m, part)
            if at:
                main = main * whole_w
            out_ref[:, at + c * QUART : at + (c + 1) * QUART] = main.astype(BF16)
            tail = tail + _dot(quarter_m[c], part)
        if at:
            tail = tail * quarter_w
        out_ref[:, at + D : at + MSG] = tail.astype(BF16)


def _send(ids, weight, tokens, cotangent):
    return pl.pallas_call(
        _send_kernel,
        in_specs=[pl.BlockSpec(memory_space=pltpu.HBM)] * 4,
        out_shape=jax.ShapeDtypeStruct((ROWS, 2 * MSG), BF16),
        scratch_shapes=[pltpu.VMEM((1, TOK), jnp.int32), pltpu.VMEM((1, TOK), F32)]
        + [pltpu.VMEM((TOK, D), BF16)] * 2
        + [pltpu.SemaphoreType.DMA((4,))],
        compiler_params=pltpu.CompilerParams(vmem_limit_bytes=VMEM_LIMIT),
        cost_estimate=pl.CostEstimate(flops=2**28, bytes_accessed=5 * 2**19, transcendentals=0),
        name="send",
    )(ids, weight, tokens, cotangent)


def _take_kernel(ids_ref, weight_ref, back_ref, out_ref, grad_ref):
    whole, quarters = _placing(ids_ref[...])
    weight = weight_ref[...]
    whole_w = _row_weights(whole, weight)
    quarter_w = sum(_row_weights(q, weight) for q in quarters)
    whole_m = whole.astype(F32).T.astype(BF16)
    quarter_m = [q.astype(F32).T.astype(BF16) for q in quarters]
    for at, ref in ((0, out_ref), (MSG, grad_ref)):
        tail = back_ref[:, at + D : at + MSG]
        if not at:
            tail = (tail.astype(F32) * quarter_w).astype(BF16)
        for c in range(4):
            main = back_ref[:, at + c * QUART : at + (c + 1) * QUART]
            if not at:
                main = (main.astype(F32) * whole_w).astype(BF16)
            both = _dot(whole_m, main) + _dot(quarter_m[c], tail)
            ref[:, c * QUART : (c + 1) * QUART] = both.astype(BF16)


def _take(ids, weight, back):
    return pl.pallas_call(
        _take_kernel,
        out_shape=[jax.ShapeDtypeStruct((TOK, D), BF16)] * 2,
        compiler_params=pltpu.CompilerParams(vmem_limit_bytes=32 * 2**20),
        cost_estimate=pl.CostEstimate(flops=2**28, bytes_accessed=5 * 2**19, transcendentals=0),
        name="take",
    )(ids, weight, back)


def _tail_row(shape, row_dim, c):
    slot, row = _iota(shape, 1 - row_dim), _iota(shape, row_dim)
    mask = row == (slot // 4) * FULL + (slot % 4) * 4 + c
    return mask.astype(F32).astype(BF16)


def _column(ref, block, rows):
    return ref.at[rows, pl.ds(pl.multiple_of(block * 128, 128), 128)]


def _expert_kernel(pos_ref, a_ref, b_ref, *refs):
    pieces = refs[:8]
    oa_ref, ob_ref, h_ref, xt_ref, xg_ref, w_ref, sems = refs[8:]
    y, x = pos_ref[0], pos_ref[1]
    copies = []
    for half in range(2):
        for outer in range(4):
            for inner in range(4):
                dy, dx = (inner, outer) if half == 0 else (outer, inner)
                block = lax.rem(y + 4 - dy, 4) * 4 + lax.rem(x + 4 - dx, 4)
                copy = pltpu.make_async_copy(
                    pieces[half * 4 + outer].at[inner],
                    _column(w_ref, block, pl.ds(half * 3 * HS, 3 * HS)),
                    sems.at[len(copies)],
                )
                copy.start()
                copies.append(copy)
    for i, ref in enumerate((a_ref, b_ref)):
        for at, x_ref in ((0, xt_ref), (MSG, xg_ref)):
            x_ref[i * ROWS : (i + 1) * ROWS, :] = ref[:, at : at + D]
            tail = ref[:, at + D : at + MSG]
            for c in range(4):
                x_ref[2 * ROWS + i * TAIL : 2 * ROWS + (i + 1) * TAIL, c * QUART : (c + 1) * QUART] = (
                    _dot(_tail_row((TAIL, ROWS), 1, c), tail).astype(BF16)
                )
    for half in range(2):
        for copy in copies[half * 16 : half * 16 + 16]:
            copy.wait()
        base = half * 3 * HS
        gate_up = _dot_nt(xt_ref[...], w_ref[base : base + 2 * HS, :])
        hidden_grad = _dot_nt(xg_ref[...], w_ref[base + 2 * HS : base + 3 * HS, :])
        gate, up = gate_up[:, :HS], gate_up[:, HS:]
        sig = jax.nn.sigmoid(gate)
        silu = gate * sig
        h_ref[:, base : base + HS] = (
            hidden_grad * up * (sig * (1.0 + gate * (1.0 - sig)))
        ).astype(BF16)
        h_ref[:, base + HS : base + 2 * HS] = (hidden_grad * silu).astype(BF16)
        h_ref[:, base + 2 * HS : base + 3 * HS] = (silu * up).astype(BF16)
    for at, first, last in ((0, 2 * HS, 3 * HS), (MSG, 0, 2 * HS)):
        own, side = slice(first, last), slice(3 * HS + first, 3 * HS + last)
        tails = [jnp.zeros((ROWS, QUART), F32), jnp.zeros((ROWS, QUART), F32)]
        for c in range(4):
            cols = slice(c * QUART, (c + 1) * QUART)
            y = _dot(h_ref[:, own], w_ref[own, cols]) + _dot(h_ref[:, side], w_ref[side, cols])
            y = y.astype(BF16)
            for i, ref in enumerate((oa_ref, ob_ref)):
                ref[:, at + c * QUART : at + (c + 1) * QUART] = y[i * ROWS : (i + 1) * ROWS]
                tail = y[2 * ROWS + i * TAIL : 2 * ROWS + (i + 1) * TAIL]
                tails[i] = tails[i] + _dot(_tail_row((ROWS, TAIL), 0, c), tail)
        for i, ref in enumerate((oa_ref, ob_ref)):
            ref[:, at + D : at + MSG] = tails[i].astype(BF16)


def _expert(pos, a, b, pieces):
    vmem = pl.BlockSpec(memory_space=pltpu.VMEM)
    return pl.pallas_call(
        _expert_kernel,
        in_specs=[pl.BlockSpec(memory_space=pltpu.SMEM)] + [vmem] * 2
        + [pl.BlockSpec(memory_space=pl.ANY)] * 8,
        out_specs=[vmem] * 5,
        out_shape=[jax.ShapeDtypeStruct((ROWS, 2 * MSG), BF16)] * 2
        + [jax.ShapeDtypeStruct((SLOTS, 6 * HS), BF16)]
        + [jax.ShapeDtypeStruct((SLOTS, D), BF16)] * 2,
        scratch_shapes=[pltpu.VMEM((6 * HS, D), BF16), pltpu.SemaphoreType.DMA((32,))],
        compiler_params=pltpu.CompilerParams(vmem_limit_bytes=VMEM_LIMIT),
        cost_estimate=pl.CostEstimate(
            flops=24 * SLOTS * HS * D, bytes_accessed=16 * 2**20, transcendentals=2 * SLOTS * HS
        ),
        name="expert",
    )(pos, a, b, *pieces)


def _terms_kernel(pos_ref, h_ref, t_ref, g_ref, *refs):
    outs, (turned, held, sems) = refs[:8], refs[8:]
    y, x = pos_ref[0], pos_ref[1]
    for i in range(6):
        rows = slice(i * HS, (i + 1) * HS)
        turned[rows, :] = h_ref[:, rows].astype(F32).T.astype(BF16)
    copies = []
    for dy in range(4):
        cols = pl.ds(pl.multiple_of(lax.rem(y + dy, 4) * QUART, QUART), QUART)
        for half in range(2):
            base = half * 3 * HS
            gate_up = _dot(turned[base : base + 2 * HS, :], t_ref[:, cols]).astype(BF16)
            down = _dot(turned[base + 2 * HS : base + 3 * HS, :], g_ref[:, cols]).astype(BF16)
            for col in range(4):
                lanes = slice(col * 128, (col + 1) * 128)
                held[half, dy * 4 + col, : 2 * HS, :] = gate_up[:, lanes]
                held[half, dy * 4 + col, 2 * HS :, :] = down[:, lanes]
            for dx in range(4):
                out = outs[dx].at[dy] if half == 0 else outs[4 + dy].at[dx]
                copy = pltpu.make_async_copy(
                    held.at[half, dy * 4 + lax.rem(x + dx, 4)], out, sems.at[len(copies)]
                )
                copy.start()
                copies.append(copy)
    for copy in copies:
        copy.wait()


def _terms(pos, h, t, g):
    vmem = pl.BlockSpec(memory_space=pltpu.VMEM)
    return pl.pallas_call(
        _terms_kernel,
        in_specs=[pl.BlockSpec(memory_space=pltpu.SMEM)] + [vmem] * 3,
        out_specs=[pl.BlockSpec(memory_space=pltpu.HBM)] * 8,
        out_shape=[jax.ShapeDtypeStruct((4, 3 * HS, 128), BF16)] * 8,
        scratch_shapes=[
            pltpu.VMEM((6 * HS, SLOTS), BF16),
            pltpu.VMEM((2, 16, 3 * HS, 128), BF16),
            pltpu.SemaphoreType.DMA((32,)),
        ],
        compiler_params=pltpu.CompilerParams(vmem_limit_bytes=VMEM_LIMIT),
        cost_estimate=pl.CostEstimate(
            flops=12 * SLOTS * HS * D, bytes_accessed=10 * 2**20, transcendentals=0
        ),
        name="terms",
    )(pos, h, t, g)


def _shift(x, axis, d):
    return lax.ppermute(x, axis, [(i, (i + d) % 4) for i in range(4)])


def _gather_pieces(piece, first, second):
    got = {d: _shift(piece, first, d) for d in (2, 1, 3)}
    stack = jnp.stack([piece, got[1], got[2], got[3]])
    got = {d: _shift(stack, second, d) for d in (2, 1, 3)}
    return [stack, got[1], got[2], got[3]]


def _sum(parts):
    return sum(p.astype(F32) for p in parts)


def _scatter_terms(parts, first, second):
    half = _sum([parts[0]] + [_shift(parts[d], first, d) for d in (2, 1, 3)]).astype(BF16)
    return _sum([half[0]] + [_shift(half[d], second, d) for d in (2, 1, 3)])


def _exchange(x):
    return lax.all_to_all(
        x.reshape(8, FULL, 2 * MSG), "pair", split_axis=0, concat_axis=0, tiled=True
    ).reshape(ROWS, 2 * MSG)


def _add(a, b):
    return (a.astype(F32) + b.astype(F32)).astype(BF16)


def local(tokens, expert_ids, route_weight, cotangent, w_gate, w_up, w_down):
    ids = expert_ids.reshape(1, TOK)
    weight = route_weight.reshape(1, TOK)
    pos = jnp.stack([lax.axis_index("y"), lax.axis_index("x")]).astype(jnp.int32)
    own_piece = _pack(w_gate, w_up, w_down)
    side_piece = lax.ppermute(own_piece, "side", SWAP)
    sent = _send(ids, weight, tokens, cotangent)
    sent, side_piece = lax.optimization_barrier((sent, side_piece))
    pieces = _gather_pieces(own_piece, "y", "x") + _gather_pieces(side_piece, "x", "y")
    own, *pieces = lax.optimization_barrier((_exchange(sent), *pieces))
    from_core = lax.ppermute(own, "core", SWAP)
    out_own, out_core, h, t, g = _expert(pos, own, from_core, pieces)
    terms = _terms(pos, h, t, g)
    back, *terms = lax.optimization_barrier((lax.ppermute(out_core, "core", SWAP), *terms))
    total = _add(out_own, back)
    own_terms = _scatter_terms(terms[:4], "x", "y")
    side_terms = _scatter_terms(terms[4:], "y", "x").astype(BF16)
    grads = (own_terms + lax.ppermute(side_terms, "side", SWAP).astype(F32)).astype(BF16)
    layer_out, token_grad = _take(ids, weight, _exchange(total))
    return layer_out, token_grad, grads[:HS], grads[HS : 2 * HS], grads[2 * HS :]


def solution(mesh):
    fine = Mesh(mesh.devices.reshape(4, 4, 8, 2, 2), ALL)
    return jax.shard_map(
        local,
        mesh=fine,
        in_specs=(P(ALL, None),) * 4 + (P(EXPERT, DP),) * 3,
        out_specs=(P(ALL, None),) * 2 + (P(EXPERT, DP),) * 3,
        check_vma=False,
    )
```

```python
import jax
import jax.numpy as jnp
from jax import lax
from jax.experimental import pallas as pl
from jax.experimental.pallas import tpu as pltpu
from jax.sharding import Mesh
from jax.sharding import PartitionSpec as P

BF16 = jnp.bfloat16
F32 = jnp.float32

D = 2048
HS = 256
TOK = 128
FULL = 16
QUART = D // 4
MSG = D + QUART
ROWS = 8 * FULL
TAIL = 32
SLOTS = 2 * (ROWS + TAIL)

ALL = ("y", "x", "pair", "side", "core")
DP = ("y", "x")
EXPERT = ("pair", "side", "core")
SWAP = [(0, 1), (1, 0)]

VMEM_LIMIT = 60 * 2**20


def _iota(shape, dim):
    return lax.broadcasted_iota(jnp.int32, shape, dim)


def _dot(a, b):
    return lax.dot_general(a, b, (((1,), (0,)), ((), ())), preferred_element_type=F32)


def _dot_nt(a, b):
    return lax.dot_general(a, b, (((1,), (1,)), ((), ())), preferred_element_type=F32)


def _dot_tn(a, b):
    return lax.dot_general(a, b, (((0,), (0,)), ((), ())), preferred_element_type=F32)


def _placing(ids):
    onehot = (ids == _iota((16, TOK), 0)).astype(F32)
    earlier = (_iota((TOK, TOK), 0) < _iota((TOK, TOK), 1)).astype(F32).astype(BF16)
    before = _dot(onehot.astype(BF16), earlier)
    rank = jnp.sum(before * onehot, axis=0, keepdims=True).astype(jnp.int32)
    row = _iota((ROWS, TOK), 0)
    whole = row == jnp.where(rank < FULL, ids * FULL + rank, -1)
    first = jnp.where(rank < FULL, -8, ids * FULL + (rank - FULL) * 4)
    quarters = [row == first + c for c in range(4)]
    return whole, quarters


def _row_weights(mask, weight):
    return jnp.sum(jnp.where(mask, weight, 0.0), axis=1, keepdims=True)


def _pack_kernel(gate_ref, up_ref, down_ref, out_ref, sems):
    copies = [
        pltpu.make_async_copy(ref, out_ref.at[pl.ds(i * HS, HS), :], sems.at[i])
        for i, ref in enumerate((gate_ref, up_ref, down_ref))
    ]
    for copy in copies:
        copy.start()
    for copy in copies:
        copy.wait()


def _pack(gate, up, down):
    return pl.pallas_call(
        _pack_kernel,
        in_specs=[pl.BlockSpec(memory_space=pltpu.HBM)] * 3,
        out_specs=pl.BlockSpec(memory_space=pltpu.VMEM),
        out_shape=jax.ShapeDtypeStruct((3 * HS, 128), BF16),
        scratch_shapes=[pltpu.SemaphoreType.DMA((3,))],
        compiler_params=pltpu.CompilerParams(vmem_limit_bytes=VMEM_LIMIT),
        cost_estimate=pl.CostEstimate(flops=0, bytes_accessed=3 * 2**17, transcendentals=0),
        name="pack",
    )(gate, up, down)


def _send_kernel(*refs):
    hbm, out_ref, held, sems = refs[:4], refs[4], refs[5:9], refs[9]
    ids_ref, weight_ref, tokens_ref, cot_ref = held
    copies = [pltpu.make_async_copy(hbm[i], held[i], sems.at[i]) for i in range(4)]
    for copy in copies:
        copy.start()
    copies[0].wait()
    copies[1].wait()
    whole, quarters = _placing(ids_ref[...])
    weight = weight_ref[...]
    whole_w = _row_weights(whole, weight)
    quarter_w = sum(_row_weights(q, weight) for q in quarters)
    whole_m = whole.astype(F32).astype(BF16)
    quarter_m = [q.astype(F32).astype(BF16) for q in quarters]
    for at, ref, copy in ((0, tokens_ref, copies[2]), (MSG, cot_ref, copies[3])):
        copy.wait()
        tail = jnp.zeros((ROWS, QUART), F32)
        for c in range(4):
            part = ref[:, c * QUART : (c + 1) * QUART]
            main = _dot(whole_m, part)
            if at:
                main = main * whole_w
            out_ref[:, at + c * QUART : at + (c + 1) * QUART] = main.astype(BF16)
            tail = tail + _dot(quarter_m[c], part)
        if at:
            tail = tail * quarter_w
        out_ref[:, at + D : at + MSG] = tail.astype(BF16)


def _send(ids, weight, tokens, cotangent):
    return pl.pallas_call(
        _send_kernel,
        in_specs=[pl.BlockSpec(memory_space=pltpu.HBM)] * 4,
        out_shape=jax.ShapeDtypeStruct((ROWS, 2 * MSG), BF16),
        scratch_shapes=[pltpu.VMEM((1, TOK), jnp.int32), pltpu.VMEM((1, TOK), F32)]
        + [pltpu.VMEM((TOK, D), BF16)] * 2
        + [pltpu.SemaphoreType.DMA((4,))],
        compiler_params=pltpu.CompilerParams(vmem_limit_bytes=VMEM_LIMIT),
        cost_estimate=pl.CostEstimate(flops=2**28, bytes_accessed=5 * 2**19, transcendentals=0),
        name="send",
    )(ids, weight, tokens, cotangent)


def _take_kernel(ids_ref, weight_ref, back_ref, out_ref, grad_ref):
    whole, quarters = _placing(ids_ref[...])
    weight = weight_ref[...]
    whole_w = _row_weights(whole, weight)
    quarter_w = sum(_row_weights(q, weight) for q in quarters)
    whole_m = whole.astype(F32).T.astype(BF16)
    quarter_m = [q.astype(F32).T.astype(BF16) for q in quarters]
    for at, ref in ((0, out_ref), (MSG, grad_ref)):
        tail = back_ref[:, at + D : at + MSG]
        if not at:
            tail = (tail.astype(F32) * quarter_w).astype(BF16)
        for c in range(4):
            main = back_ref[:, at + c * QUART : at + (c + 1) * QUART]
            if not at:
                main = (main.astype(F32) * whole_w).astype(BF16)
            both = _dot(whole_m, main) + _dot(quarter_m[c], tail)
            ref[:, c * QUART : (c + 1) * QUART] = both.astype(BF16)


def _take(ids, weight, back):
    return pl.pallas_call(
        _take_kernel,
        out_shape=[jax.ShapeDtypeStruct((TOK, D), BF16)] * 2,
        compiler_params=pltpu.CompilerParams(vmem_limit_bytes=32 * 2**20),
        cost_estimate=pl.CostEstimate(flops=2**28, bytes_accessed=5 * 2**19, transcendentals=0),
        name="take",
    )(ids, weight, back)


def _tail_row(shape, row_dim, c):
    slot, row = _iota(shape, 1 - row_dim), _iota(shape, row_dim)
    mask = row == (slot // 4) * FULL + (slot % 4) * 4 + c
    return mask.astype(F32).astype(BF16)


def _column(ref, block, rows):
    return ref.at[rows, pl.ds(pl.multiple_of(block * 128, 128), 128)]


def _expert_kernel(pos_ref, a_ref, b_ref, *refs):
    pieces = refs[:8]
    oa_ref, ob_ref, h_ref, xt_ref, xg_ref, w_ref, sems = refs[8:]
    y, x = pos_ref[0], pos_ref[1]
    copies = []
    for half in range(2):
        for outer in range(4):
            for inner in range(4):
                dy, dx = (inner, outer) if half == 0 else (outer, inner)
                block = lax.rem(y + 4 - dy, 4) * 4 + lax.rem(x + 4 - dx, 4)
                copy = pltpu.make_async_copy(
                    pieces[half * 4 + outer].at[inner],
                    _column(w_ref, block, pl.ds(half * 3 * HS, 3 * HS)),
                    sems.at[len(copies)],
                )
                copy.start()
                copies.append(copy)
    for i, ref in enumerate((a_ref, b_ref)):
        for at, x_ref in ((0, xt_ref), (MSG, xg_ref)):
            x_ref[i * ROWS : (i + 1) * ROWS, :] = ref[:, at : at + D]
            tail = ref[:, at + D : at + MSG]
            for c in range(4):
                x_ref[2 * ROWS + i * TAIL : 2 * ROWS + (i + 1) * TAIL, c * QUART : (c + 1) * QUART] = (
                    _dot(_tail_row((TAIL, ROWS), 1, c), tail).astype(BF16)
                )
    for half in range(2):
        for copy in copies[half * 16 : half * 16 + 16]:
            copy.wait()
        base = half * 3 * HS
        gate_up = _dot_nt(xt_ref[...], w_ref[base : base + 2 * HS, :])
        hidden_grad = _dot_nt(xg_ref[...], w_ref[base + 2 * HS : base + 3 * HS, :])
        gate, up = gate_up[:, :HS], gate_up[:, HS:]
        sig = jax.nn.sigmoid(gate)
        silu = gate * sig
        h_ref[:, base : base + HS] = (
            hidden_grad * up * (sig * (1.0 + gate * (1.0 - sig)))
        ).astype(BF16)
        h_ref[:, base + HS : base + 2 * HS] = (hidden_grad * silu).astype(BF16)
        h_ref[:, base + 2 * HS : base + 3 * HS] = (silu * up).astype(BF16)
    for at, first, last in ((0, 2 * HS, 3 * HS), (MSG, 0, 2 * HS)):
        own, side = slice(first, last), slice(3 * HS + first, 3 * HS + last)
        tails = [jnp.zeros((ROWS, QUART), F32), jnp.zeros((ROWS, QUART), F32)]
        for c in range(4):
            cols = slice(c * QUART, (c + 1) * QUART)
            y = _dot(h_ref[:, own], w_ref[own, cols]) + _dot(h_ref[:, side], w_ref[side, cols])
            y = y.astype(BF16)
            for i, ref in enumerate((oa_ref, ob_ref)):
                ref[:, at + c * QUART : at + (c + 1) * QUART] = y[i * ROWS : (i + 1) * ROWS]
                tail = y[2 * ROWS + i * TAIL : 2 * ROWS + (i + 1) * TAIL]
                tails[i] = tails[i] + _dot(_tail_row((ROWS, TAIL), 0, c), tail)
        for i, ref in enumerate((oa_ref, ob_ref)):
            ref[:, at + D : at + MSG] = tails[i].astype(BF16)


def _expert(pos, a, b, pieces):
    vmem = pl.BlockSpec(memory_space=pltpu.VMEM)
    return pl.pallas_call(
        _expert_kernel,
        in_specs=[pl.BlockSpec(memory_space=pltpu.SMEM)] + [vmem] * 2
        + [pl.BlockSpec(memory_space=pl.ANY)] * 8,
        out_specs=[vmem] * 5,
        out_shape=[jax.ShapeDtypeStruct((ROWS, 2 * MSG), BF16)] * 2
        + [jax.ShapeDtypeStruct((SLOTS, 6 * HS), BF16)]
        + [jax.ShapeDtypeStruct((SLOTS, D), BF16)] * 2,
        scratch_shapes=[pltpu.VMEM((6 * HS, D), BF16), pltpu.SemaphoreType.DMA((32,))],
        compiler_params=pltpu.CompilerParams(vmem_limit_bytes=VMEM_LIMIT),
        cost_estimate=pl.CostEstimate(
            flops=24 * SLOTS * HS * D, bytes_accessed=16 * 2**20, transcendentals=2 * SLOTS * HS
        ),
        name="expert",
    )(pos, a, b, *pieces)


def _terms_kernel(pos_ref, h_ref, t_ref, g_ref, *refs):
    outs, (turned, held, sems) = refs[:8], refs[8:]
    y, x = pos_ref[0], pos_ref[1]
    for i in range(6):
        rows = slice(i * HS, (i + 1) * HS)
        turned[rows, :] = h_ref[:, rows].astype(F32).T.astype(BF16)
    copies = []
    for dy in range(4):
        cols = pl.ds(pl.multiple_of(lax.rem(y + dy, 4) * QUART, QUART), QUART)
        for half in range(2):
            base = half * 3 * HS
            gate_up = _dot(turned[base : base + 2 * HS, :], t_ref[:, cols]).astype(BF16)
            down = _dot(turned[base + 2 * HS : base + 3 * HS, :], g_ref[:, cols]).astype(BF16)
            for col in range(4):
                lanes = slice(col * 128, (col + 1) * 128)
                held[half, dy * 4 + col, : 2 * HS, :] = gate_up[:, lanes]
                held[half, dy * 4 + col, 2 * HS :, :] = down[:, lanes]
            for dx in range(4):
                out = outs[dx].at[dy] if half == 0 else outs[4 + dy].at[dx]
                copy = pltpu.make_async_copy(
                    held.at[half, dy * 4 + lax.rem(x + dx, 4)], out, sems.at[len(copies)]
                )
                copy.start()
                copies.append(copy)
    for copy in copies:
        copy.wait()


def _terms(pos, h, t, g):
    vmem = pl.BlockSpec(memory_space=pltpu.VMEM)
    return pl.pallas_call(
        _terms_kernel,
        in_specs=[pl.BlockSpec(memory_space=pltpu.SMEM)] + [vmem] * 3,
        out_specs=[pl.BlockSpec(memory_space=pltpu.HBM)] * 8,
        out_shape=[jax.ShapeDtypeStruct((4, 3 * HS, 128), BF16)] * 8,
        scratch_shapes=[
            pltpu.VMEM((6 * HS, SLOTS), BF16),
            pltpu.VMEM((2, 16, 3 * HS, 128), BF16),
            pltpu.SemaphoreType.DMA((32,)),
        ],
        compiler_params=pltpu.CompilerParams(vmem_limit_bytes=VMEM_LIMIT),
        cost_estimate=pl.CostEstimate(
            flops=12 * SLOTS * HS * D, bytes_accessed=10 * 2**20, transcendentals=0
        ),
        name="terms",
    )(pos, h, t, g)


def _shift(x, axis, d):
    return lax.ppermute(x, axis, [(i, (i + d) % 4) for i in range(4)])


def _gather_near(piece, axis):
    got = {d: _shift(piece, axis, d) for d in (2, 1, 3)}
    return jnp.stack([piece, got[1], got[2], got[3]])


def _gather_far(stack, axis):
    got = {d: _shift(stack, axis, d) for d in (2, 1, 3)}
    return [stack, got[1], got[2], got[3]]


def _sum(parts):
    return sum(p.astype(F32) for p in parts)


def _scatter_terms(parts, first, second):
    half = _sum([parts[0]] + [_shift(parts[d], first, d) for d in (2, 1, 3)]).astype(BF16)
    return _sum([half[0]] + [_shift(half[d], second, d) for d in (2, 1, 3)])


def _exchange(x):
    return lax.all_to_all(
        x.reshape(8, FULL, 2 * MSG), "pair", split_axis=0, concat_axis=0, tiled=True
    ).reshape(ROWS, 2 * MSG)


def _add(a, b):
    return (a.astype(F32) + b.astype(F32)).astype(BF16)


def local(tokens, expert_ids, route_weight, cotangent, w_gate, w_up, w_down):
    ids = expert_ids.reshape(1, TOK)
    weight = route_weight.reshape(1, TOK)
    pos = jnp.stack([lax.axis_index("y"), lax.axis_index("x")]).astype(jnp.int32)
    own_piece = _pack(w_gate, w_up, w_down)
    side_piece = lax.ppermute(own_piece, "side", SWAP)
    sent = _send(ids, weight, tokens, cotangent)
    sent, side_piece = lax.optimization_barrier((sent, side_piece))
    own_stack, side_stack = lax.optimization_barrier(
        (_gather_near(own_piece, "y"), _gather_near(side_piece, "x"))
    )
    pieces = _gather_far(own_stack, "x") + _gather_far(side_stack, "y")
    own, *pieces = lax.optimization_barrier((_exchange(sent), *pieces))
    from_core = lax.ppermute(own, "core", SWAP)
    out_own, out_core, h, t, g = _expert(pos, own, from_core, pieces)
    terms = _terms(pos, h, t, g)
    back, *terms = lax.optimization_barrier((lax.ppermute(out_core, "core", SWAP), *terms))
    total = _add(out_own, back)
    own_terms = _scatter_terms(terms[:4], "x", "y")
    side_terms = _scatter_terms(terms[4:], "y", "x").astype(BF16)
    grads = (own_terms + lax.ppermute(side_terms, "side", SWAP).astype(F32)).astype(BF16)
    layer_out, token_grad = _take(ids, weight, _exchange(total))
    return layer_out, token_grad, grads[:HS], grads[HS : 2 * HS], grads[2 * HS :]


def solution(mesh):
    fine = Mesh(mesh.devices.reshape(4, 4, 8, 2, 2), ALL)
    return jax.shard_map(
        local,
        mesh=fine,
        in_specs=(P(ALL, None),) * 4 + (P(EXPERT, DP),) * 3,
        out_specs=(P(ALL, None),) * 2 + (P(EXPERT, DP),) * 3,
        check_vma=False,
    )
```

```python
import jax
import jax.numpy as jnp
from jax import lax
from jax.experimental import pallas as pl
from jax.experimental.pallas import tpu as pltpu
from jax.sharding import Mesh
from jax.sharding import PartitionSpec as P

BF16 = jnp.bfloat16
F32 = jnp.float32

D = 2048
HS = 256
TOK = 128
FULL = 16
QUART = D // 4
MSG = D + QUART
ROWS = 8 * FULL
TAIL = 32
SLOTS = 2 * (ROWS + TAIL)

ALL = ("y", "x", "pair", "side", "core")
DP = ("y", "x")
EXPERT = ("pair", "side", "core")
SWAP = [(0, 1), (1, 0)]

VMEM_LIMIT = 60 * 2**20


def _iota(shape, dim):
    return lax.broadcasted_iota(jnp.int32, shape, dim)


def _dot(a, b):
    return lax.dot_general(a, b, (((1,), (0,)), ((), ())), preferred_element_type=F32)


def _dot_nt(a, b):
    return lax.dot_general(a, b, (((1,), (1,)), ((), ())), preferred_element_type=F32)


def _dot_tn(a, b):
    return lax.dot_general(a, b, (((0,), (0,)), ((), ())), preferred_element_type=F32)


def _placing(ids):
    onehot = (ids == _iota((16, TOK), 0)).astype(F32)
    earlier = (_iota((TOK, TOK), 0) < _iota((TOK, TOK), 1)).astype(F32).astype(BF16)
    before = _dot(onehot.astype(BF16), earlier)
    rank = jnp.sum(before * onehot, axis=0, keepdims=True).astype(jnp.int32)
    row = _iota((ROWS, TOK), 0)
    whole = row == jnp.where(rank < FULL, ids * FULL + rank, -1)
    first = jnp.where(rank < FULL, -8, ids * FULL + (rank - FULL) * 4)
    quarters = [row == first + c for c in range(4)]
    return whole, quarters


def _row_weights(mask, weight):
    return jnp.sum(jnp.where(mask, weight, 0.0), axis=1, keepdims=True)


def _pack_kernel(gate_ref, up_ref, down_ref, out_ref, sems):
    copies = [
        pltpu.make_async_copy(ref, out_ref.at[pl.ds(i * HS, HS), :], sems.at[i])
        for i, ref in enumerate((gate_ref, up_ref, down_ref))
    ]
    for copy in copies:
        copy.start()
    for copy in copies:
        copy.wait()


def _pack(gate, up, down):
    return pl.pallas_call(
        _pack_kernel,
        in_specs=[pl.BlockSpec(memory_space=pltpu.HBM)] * 3,
        out_specs=pl.BlockSpec(memory_space=pltpu.VMEM),
        out_shape=jax.ShapeDtypeStruct((3 * HS, 128), BF16),
        scratch_shapes=[pltpu.SemaphoreType.DMA((3,))],
        compiler_params=pltpu.CompilerParams(vmem_limit_bytes=VMEM_LIMIT),
        cost_estimate=pl.CostEstimate(flops=0, bytes_accessed=3 * 2**17, transcendentals=0),
        name="pack",
    )(gate, up, down)


def _send_kernel(*refs):
    hbm, out_ref, held, sems = refs[:4], refs[4], refs[5:9], refs[9]
    ids_ref, weight_ref, tokens_ref, cot_ref = held
    copies = [pltpu.make_async_copy(hbm[i], held[i], sems.at[i]) for i in range(4)]
    for copy in copies:
        copy.start()
    copies[0].wait()
    copies[1].wait()
    whole, quarters = _placing(ids_ref[...])
    weight = weight_ref[...]
    whole_w = _row_weights(whole, weight)
    quarter_w = sum(_row_weights(q, weight) for q in quarters)
    whole_m = whole.astype(F32).astype(BF16)
    quarter_m = [q.astype(F32).astype(BF16) for q in quarters]
    for at, ref, copy in ((0, tokens_ref, copies[2]), (MSG, cot_ref, copies[3])):
        copy.wait()
        tail = jnp.zeros((ROWS, QUART), F32)
        for c in range(4):
            part = ref[:, c * QUART : (c + 1) * QUART]
            main = _dot(whole_m, part)
            if at:
                main = main * whole_w
            out_ref[:, at + c * QUART : at + (c + 1) * QUART] = main.astype(BF16)
            tail = tail + _dot(quarter_m[c], part)
        if at:
            tail = tail * quarter_w
        out_ref[:, at + D : at + MSG] = tail.astype(BF16)


def _send(ids, weight, tokens, cotangent):
    return pl.pallas_call(
        _send_kernel,
        in_specs=[pl.BlockSpec(memory_space=pltpu.HBM)] * 4,
        out_shape=jax.ShapeDtypeStruct((ROWS, 2 * MSG), BF16),
        scratch_shapes=[pltpu.VMEM((1, TOK), jnp.int32), pltpu.VMEM((1, TOK), F32)]
        + [pltpu.VMEM((TOK, D), BF16)] * 2
        + [pltpu.SemaphoreType.DMA((4,))],
        compiler_params=pltpu.CompilerParams(vmem_limit_bytes=VMEM_LIMIT),
        cost_estimate=pl.CostEstimate(flops=2**28, bytes_accessed=5 * 2**19, transcendentals=0),
        name="send",
    )(ids, weight, tokens, cotangent)


def _take_kernel(ids_ref, weight_ref, back_ref, out_ref, grad_ref):
    whole, quarters = _placing(ids_ref[...])
    weight = weight_ref[...]
    whole_w = _row_weights(whole, weight)
    quarter_w = sum(_row_weights(q, weight) for q in quarters)
    whole_m = whole.astype(F32).T.astype(BF16)
    quarter_m = [q.astype(F32).T.astype(BF16) for q in quarters]
    for at, ref in ((0, out_ref), (MSG, grad_ref)):
        tail = back_ref[:, at + D : at + MSG]
        if not at:
            tail = (tail.astype(F32) * quarter_w).astype(BF16)
        for c in range(4):
            main = back_ref[:, at + c * QUART : at + (c + 1) * QUART]
            if not at:
                main = (main.astype(F32) * whole_w).astype(BF16)
            both = _dot(whole_m, main) + _dot(quarter_m[c], tail)
            ref[:, c * QUART : (c + 1) * QUART] = both.astype(BF16)


def _take(ids, weight, back):
    return pl.pallas_call(
        _take_kernel,
        out_shape=[jax.ShapeDtypeStruct((TOK, D), BF16)] * 2,
        compiler_params=pltpu.CompilerParams(vmem_limit_bytes=32 * 2**20),
        cost_estimate=pl.CostEstimate(flops=2**28, bytes_accessed=5 * 2**19, transcendentals=0),
        name="take",
    )(ids, weight, back)


def _tail_row(shape, row_dim, c):
    slot, row = _iota(shape, 1 - row_dim), _iota(shape, row_dim)
    mask = row == (slot // 4) * FULL + (slot % 4) * 4 + c
    return mask.astype(F32).astype(BF16)


def _column(ref, block, rows):
    return ref.at[rows, pl.ds(pl.multiple_of(block * 128, 128), 128)]


def _expert_kernel(pos_ref, a_ref, b_ref, *refs):
    pieces = refs[:8]
    oa_ref, ob_ref, h_ref, xt_ref, xg_ref, w_ref, sems = refs[8:]
    y, x = pos_ref[0], pos_ref[1]
    copies = []
    for half in range(2):
        for outer in range(4):
            for inner in range(4):
                dy, dx = (inner, outer) if half == 0 else (outer, inner)
                block = lax.rem(y + 4 - dy, 4) * 4 + lax.rem(x + 4 - dx, 4)
                copy = pltpu.make_async_copy(
                    pieces[half * 4 + outer].at[inner],
                    _column(w_ref, block, pl.ds(half * 3 * HS, 3 * HS)),
                    sems.at[len(copies)],
                )
                copy.start()
                copies.append(copy)
    for i, ref in enumerate((a_ref, b_ref)):
        for at, x_ref in ((0, xt_ref), (MSG, xg_ref)):
            x_ref[i * ROWS : (i + 1) * ROWS, :] = ref[:, at : at + D]
            tail = ref[:, at + D : at + MSG]
            for c in range(4):
                x_ref[2 * ROWS + i * TAIL : 2 * ROWS + (i + 1) * TAIL, c * QUART : (c + 1) * QUART] = (
                    _dot(_tail_row((TAIL, ROWS), 1, c), tail).astype(BF16)
                )
    for half in range(2):
        for copy in copies[half * 16 : half * 16 + 16]:
            copy.wait()
        base = half * 3 * HS
        gate_up = _dot_nt(xt_ref[...], w_ref[base : base + 2 * HS, :])
        hidden_grad = _dot_nt(xg_ref[...], w_ref[base + 2 * HS : base + 3 * HS, :])
        gate, up = gate_up[:, :HS], gate_up[:, HS:]
        sig = jax.nn.sigmoid(gate)
        silu = gate * sig
        h_ref[:, base : base + HS] = (
            hidden_grad * up * (sig * (1.0 + gate * (1.0 - sig)))
        ).astype(BF16)
        h_ref[:, base + HS : base + 2 * HS] = (hidden_grad * silu).astype(BF16)
        h_ref[:, base + 2 * HS : base + 3 * HS] = (silu * up).astype(BF16)
    for at, first, last in ((0, 2 * HS, 3 * HS), (MSG, 0, 2 * HS)):
        own, side = slice(first, last), slice(3 * HS + first, 3 * HS + last)
        tails = [jnp.zeros((ROWS, QUART), F32), jnp.zeros((ROWS, QUART), F32)]
        for c in range(4):
            cols = slice(c * QUART, (c + 1) * QUART)
            y = _dot(h_ref[:, own], w_ref[own, cols]) + _dot(h_ref[:, side], w_ref[side, cols])
            y = y.astype(BF16)
            for i, ref in enumerate((oa_ref, ob_ref)):
                ref[:, at + c * QUART : at + (c + 1) * QUART] = y[i * ROWS : (i + 1) * ROWS]
                tail = y[2 * ROWS + i * TAIL : 2 * ROWS + (i + 1) * TAIL]
                tails[i] = tails[i] + _dot(_tail_row((ROWS, TAIL), 0, c), tail)
        for i, ref in enumerate((oa_ref, ob_ref)):
            ref[:, at + D : at + MSG] = tails[i].astype(BF16)


def _expert(pos, a, b, pieces):
    vmem = pl.BlockSpec(memory_space=pltpu.VMEM)
    return pl.pallas_call(
        _expert_kernel,
        in_specs=[pl.BlockSpec(memory_space=pltpu.SMEM)] + [vmem] * 2
        + [pl.BlockSpec(memory_space=pl.ANY)] * 8,
        out_specs=[vmem] * 5,
        out_shape=[jax.ShapeDtypeStruct((ROWS, 2 * MSG), BF16)] * 2
        + [jax.ShapeDtypeStruct((SLOTS, 6 * HS), BF16)]
        + [jax.ShapeDtypeStruct((SLOTS, D), BF16)] * 2,
        scratch_shapes=[pltpu.VMEM((6 * HS, D), BF16), pltpu.SemaphoreType.DMA((32,))],
        compiler_params=pltpu.CompilerParams(vmem_limit_bytes=VMEM_LIMIT),
        cost_estimate=pl.CostEstimate(
            flops=24 * SLOTS * HS * D, bytes_accessed=16 * 2**20, transcendentals=2 * SLOTS * HS
        ),
        name="expert",
    )(pos, a, b, *pieces)


def _terms_kernel(pos_ref, h_ref, t_ref, g_ref, *refs):
    outs, (turned, held, sems) = refs[:8], refs[8:]
    y, x = pos_ref[0], pos_ref[1]
    for i in range(6):
        rows = slice(i * HS, (i + 1) * HS)
        turned[rows, :] = h_ref[:, rows].astype(F32).T.astype(BF16)
    copies = []
    for dy in range(4):
        cols = pl.ds(pl.multiple_of(lax.rem(y + dy, 4) * QUART, QUART), QUART)
        for half in range(2):
            base = half * 3 * HS
            gate_up = _dot(turned[base : base + 2 * HS, :], t_ref[:, cols]).astype(BF16)
            down = _dot(turned[base + 2 * HS : base + 3 * HS, :], g_ref[:, cols]).astype(BF16)
            for col in range(4):
                lanes = slice(col * 128, (col + 1) * 128)
                held[half, dy * 4 + col, : 2 * HS, :] = gate_up[:, lanes]
                held[half, dy * 4 + col, 2 * HS :, :] = down[:, lanes]
            for dx in range(4):
                out = outs[dx].at[dy] if half == 0 else outs[4 + dy].at[dx]
                copy = pltpu.make_async_copy(
                    held.at[half, dy * 4 + lax.rem(x + dx, 4)], out, sems.at[len(copies)]
                )
                copy.start()
                copies.append(copy)
    for copy in copies:
        copy.wait()


def _terms(pos, h, t, g):
    vmem = pl.BlockSpec(memory_space=pltpu.VMEM)
    return pl.pallas_call(
        _terms_kernel,
        in_specs=[pl.BlockSpec(memory_space=pltpu.SMEM)] + [vmem] * 3,
        out_specs=[pl.BlockSpec(memory_space=pltpu.HBM)] * 8,
        out_shape=[jax.ShapeDtypeStruct((4, 3 * HS, 128), BF16)] * 8,
        scratch_shapes=[
            pltpu.VMEM((6 * HS, SLOTS), BF16),
            pltpu.VMEM((2, 16, 3 * HS, 128), BF16),
            pltpu.SemaphoreType.DMA((32,)),
        ],
        compiler_params=pltpu.CompilerParams(vmem_limit_bytes=VMEM_LIMIT),
        cost_estimate=pl.CostEstimate(
            flops=12 * SLOTS * HS * D, bytes_accessed=10 * 2**20, transcendentals=0
        ),
        name="terms",
    )(pos, h, t, g)


def _shift(x, axis, d):
    return lax.ppermute(x, axis, [(i, (i + d) % 4) for i in range(4)])


def _gather_near(piece, axis):
    got = {d: _shift(piece, axis, d) for d in (2, 1, 3)}
    return jnp.stack([piece, got[1], got[2], got[3]])


def _gather_far(stack, axis):
    got = {d: _shift(stack, axis, d) for d in (2, 1, 3)}
    return [stack, got[1], got[2], got[3]]


def _sum(parts):
    return sum(p.astype(F32) for p in parts)


def _scatter_terms(parts, first, second):
    half = _sum([parts[0]] + [_shift(parts[d], first, d) for d in (2, 1, 3)]).astype(BF16)
    return _sum([half[0]] + [_shift(half[d], second, d) for d in (2, 1, 3)])


def _exchange(x):
    return lax.all_to_all(
        x.reshape(8, FULL, 2 * MSG), "pair", split_axis=0, concat_axis=0, tiled=True
    ).reshape(ROWS, 2 * MSG)


def _add(a, b):
    return (a.astype(F32) + b.astype(F32)).astype(BF16)


def local(tokens, expert_ids, route_weight, cotangent, w_gate, w_up, w_down):
    ids = expert_ids.reshape(1, TOK)
    weight = route_weight.reshape(1, TOK)
    pos = jnp.stack([lax.axis_index("y"), lax.axis_index("x")]).astype(jnp.int32)
    own_piece = _pack(w_gate, w_up, w_down)
    side_piece = lax.ppermute(own_piece, "side", SWAP)
    sent = _send(ids, weight, tokens, cotangent)
    own_stack = _gather_near(own_piece, "y")
    sent, side_piece, own_stack = lax.optimization_barrier((sent, side_piece, own_stack))
    own_stack, side_stack = lax.optimization_barrier(
        (own_stack, _gather_near(side_piece, "x"))
    )
    pieces = _gather_far(own_stack, "x") + _gather_far(side_stack, "y")
    own, *pieces = lax.optimization_barrier((_exchange(sent), *pieces))
    from_core = lax.ppermute(own, "core", SWAP)
    out_own, out_core, h, t, g = _expert(pos, own, from_core, pieces)
    terms = _terms(pos, h, t, g)
    back, *terms = lax.optimization_barrier((lax.ppermute(out_core, "core", SWAP), *terms))
    total = _add(out_own, back)
    own_terms = _scatter_terms(terms[:4], "x", "y")
    side_terms = _scatter_terms(terms[4:], "y", "x").astype(BF16)
    grads = (own_terms + lax.ppermute(side_terms, "side", SWAP).astype(F32)).astype(BF16)
    layer_out, token_grad = _take(ids, weight, _exchange(total))
    return layer_out, token_grad, grads[:HS], grads[HS : 2 * HS], grads[2 * HS :]


def solution(mesh):
    fine = Mesh(mesh.devices.reshape(4, 4, 8, 2, 2), ALL)
    return jax.shard_map(
        local,
        mesh=fine,
        in_specs=(P(ALL, None),) * 4 + (P(EXPERT, DP),) * 3,
        out_specs=(P(ALL, None),) * 2 + (P(EXPERT, DP),) * 3,
        check_vma=False,
    )
```

```python
import jax
import jax.numpy as jnp
from jax import lax
from jax.experimental import pallas as pl
from jax.experimental.pallas import tpu as pltpu
from jax.sharding import Mesh
from jax.sharding import PartitionSpec as P

BF16 = jnp.bfloat16
F32 = jnp.float32

D = 2048
HS = 256
TOK = 128
FULL = 16
QUART = D // 4
MSG = D + QUART
ROWS = 8 * FULL
TAIL = 32
SLOTS = 2 * (ROWS + TAIL)

ALL = ("y", "x", "pair", "side", "core")
DP = ("y", "x")
EXPERT = ("pair", "side", "core")
SWAP = [(0, 1), (1, 0)]

VMEM_LIMIT = 60 * 2**20


def _iota(shape, dim):
    return lax.broadcasted_iota(jnp.int32, shape, dim)


def _dot(a, b):
    return lax.dot_general(a, b, (((1,), (0,)), ((), ())), preferred_element_type=F32)


def _dot_nt(a, b):
    return lax.dot_general(a, b, (((1,), (1,)), ((), ())), preferred_element_type=F32)


def _dot_tn(a, b):
    return lax.dot_general(a, b, (((0,), (0,)), ((), ())), preferred_element_type=F32)


def _placing(ids):
    onehot = (ids == _iota((16, TOK), 0)).astype(F32)
    earlier = (_iota((TOK, TOK), 0) < _iota((TOK, TOK), 1)).astype(F32).astype(BF16)
    before = _dot(onehot.astype(BF16), earlier)
    rank = jnp.sum(before * onehot, axis=0, keepdims=True).astype(jnp.int32)
    row = _iota((ROWS, TOK), 0)
    whole = row == jnp.where(rank < FULL, ids * FULL + rank, -1)
    first = jnp.where(rank < FULL, -8, ids * FULL + (rank - FULL) * 4)
    quarters = [row == first + c for c in range(4)]
    return whole, quarters


def _row_weights(mask, weight):
    return jnp.sum(jnp.where(mask, weight, 0.0), axis=1, keepdims=True)


def _pack_kernel(gate_ref, up_ref, down_ref, out_ref, sems):
    copies = [
        pltpu.make_async_copy(ref, out_ref.at[pl.ds(i * HS, HS), :], sems.at[i])
        for i, ref in enumerate((gate_ref, up_ref, down_ref))
    ]
    for copy in copies:
        copy.start()
    for copy in copies:
        copy.wait()


def _pack(gate, up, down):
    return pl.pallas_call(
        _pack_kernel,
        in_specs=[pl.BlockSpec(memory_space=pltpu.HBM)] * 3,
        out_specs=pl.BlockSpec(memory_space=pltpu.VMEM),
        out_shape=jax.ShapeDtypeStruct((3 * HS, 128), BF16),
        scratch_shapes=[pltpu.SemaphoreType.DMA((3,))],
        compiler_params=pltpu.CompilerParams(vmem_limit_bytes=VMEM_LIMIT),
        cost_estimate=pl.CostEstimate(flops=0, bytes_accessed=3 * 2**17, transcendentals=0),
        name="pack",
    )(gate, up, down)


def _send_kernel(*refs):
    hbm, out_ref, held, sems = refs[:4], refs[4], refs[5:9], refs[9]
    ids_ref, weight_ref, tokens_ref, cot_ref = held
    copies = [pltpu.make_async_copy(hbm[i], held[i], sems.at[i]) for i in range(4)]
    for copy in copies:
        copy.start()
    copies[0].wait()
    copies[1].wait()
    whole, quarters = _placing(ids_ref[...])
    weight = weight_ref[...]
    whole_w = _row_weights(whole, weight)
    quarter_w = sum(_row_weights(q, weight) for q in quarters)
    whole_m = whole.astype(F32).astype(BF16)
    quarter_m = [q.astype(F32).astype(BF16) for q in quarters]
    for at, ref, copy in ((0, tokens_ref, copies[2]), (MSG, cot_ref, copies[3])):
        copy.wait()
        tail = jnp.zeros((ROWS, QUART), F32)
        for c in range(4):
            part = ref[:, c * QUART : (c + 1) * QUART]
            main = _dot(whole_m, part)
            if at:
                main = main * whole_w
            out_ref[:, at + c * QUART : at + (c + 1) * QUART] = main.astype(BF16)
            tail = tail + _dot(quarter_m[c], part)
        if at:
            tail = tail * quarter_w
        out_ref[:, at + D : at + MSG] = tail.astype(BF16)


def _send(ids, weight, tokens, cotangent):
    return pl.pallas_call(
        _send_kernel,
        in_specs=[pl.BlockSpec(memory_space=pltpu.HBM)] * 4,
        out_shape=jax.ShapeDtypeStruct((ROWS, 2 * MSG), BF16),
        scratch_shapes=[pltpu.VMEM((1, TOK), jnp.int32), pltpu.VMEM((1, TOK), F32)]
        + [pltpu.VMEM((TOK, D), BF16)] * 2
        + [pltpu.SemaphoreType.DMA((4,))],
        compiler_params=pltpu.CompilerParams(vmem_limit_bytes=VMEM_LIMIT),
        cost_estimate=pl.CostEstimate(flops=2**28, bytes_accessed=5 * 2**19, transcendentals=0),
        name="send",
    )(ids, weight, tokens, cotangent)


def _take_kernel(ids_ref, weight_ref, back_ref, out_ref, grad_ref):
    whole, quarters = _placing(ids_ref[...])
    weight = weight_ref[...]
    whole_w = _row_weights(whole, weight)
    quarter_w = sum(_row_weights(q, weight) for q in quarters)
    whole_m = whole.astype(F32).T.astype(BF16)
    quarter_m = [q.astype(F32).T.astype(BF16) for q in quarters]
    for at, ref in ((0, out_ref), (MSG, grad_ref)):
        tail = back_ref[:, at + D : at + MSG]
        if not at:
            tail = (tail.astype(F32) * quarter_w).astype(BF16)
        for c in range(4):
            main = back_ref[:, at + c * QUART : at + (c + 1) * QUART]
            if not at:
                main = (main.astype(F32) * whole_w).astype(BF16)
            both = _dot(whole_m, main) + _dot(quarter_m[c], tail)
            ref[:, c * QUART : (c + 1) * QUART] = both.astype(BF16)


def _take(ids, weight, back):
    return pl.pallas_call(
        _take_kernel,
        out_shape=[jax.ShapeDtypeStruct((TOK, D), BF16)] * 2,
        compiler_params=pltpu.CompilerParams(vmem_limit_bytes=32 * 2**20),
        cost_estimate=pl.CostEstimate(flops=2**28, bytes_accessed=5 * 2**19, transcendentals=0),
        name="take",
    )(ids, weight, back)


def _tail_row(shape, row_dim, c):
    slot, row = _iota(shape, 1 - row_dim), _iota(shape, row_dim)
    mask = row == (slot // 4) * FULL + (slot % 4) * 4 + c
    return mask.astype(F32).astype(BF16)


def _column(ref, block, rows):
    return ref.at[rows, pl.ds(pl.multiple_of(block * 128, 128), 128)]


def _expert_kernel(pos_ref, a_ref, b_ref, *refs):
    pieces = refs[:8]
    oa_ref, ob_ref, outs = refs[8], refs[9], refs[10:18]
    h_ref, xt_ref, xg_ref, w_ref, turned, held, sems, out_sems = refs[18:]
    y, x = pos_ref[0], pos_ref[1]
    copies = []
    for half in range(2):
        for outer in range(4):
            for inner in range(4):
                dy, dx = (inner, outer) if half == 0 else (outer, inner)
                block = lax.rem(y + 4 - dy, 4) * 4 + lax.rem(x + 4 - dx, 4)
                copy = pltpu.make_async_copy(
                    pieces[half * 4 + outer].at[inner],
                    _column(w_ref, block, pl.ds(half * 3 * HS, 3 * HS)),
                    sems.at[len(copies)],
                )
                copy.start()
                copies.append(copy)
    for i, ref in enumerate((a_ref, b_ref)):
        for at, x_ref in ((0, xt_ref), (MSG, xg_ref)):
            x_ref[i * ROWS : (i + 1) * ROWS, :] = ref[:, at : at + D]
            tail = ref[:, at + D : at + MSG]
            for c in range(4):
                x_ref[2 * ROWS + i * TAIL : 2 * ROWS + (i + 1) * TAIL, c * QUART : (c + 1) * QUART] = (
                    _dot(_tail_row((TAIL, ROWS), 1, c), tail).astype(BF16)
                )
    for half in range(2):
        for copy in copies[half * 16 : half * 16 + 16]:
            copy.wait()
        base = half * 3 * HS
        gate_up = _dot_nt(xt_ref[...], w_ref[base : base + 2 * HS, :])
        hidden_grad = _dot_nt(xg_ref[...], w_ref[base + 2 * HS : base + 3 * HS, :])
        gate, up = gate_up[:, :HS], gate_up[:, HS:]
        sig = jax.nn.sigmoid(gate)
        silu = gate * sig
        h_ref[:, base : base + HS] = (
            hidden_grad * up * (sig * (1.0 + gate * (1.0 - sig)))
        ).astype(BF16)
        h_ref[:, base + HS : base + 2 * HS] = (hidden_grad * silu).astype(BF16)
        h_ref[:, base + 2 * HS : base + 3 * HS] = (silu * up).astype(BF16)
    for at, first, last in ((0, 2 * HS, 3 * HS), (MSG, 0, 2 * HS)):
        own, side = slice(first, last), slice(3 * HS + first, 3 * HS + last)
        tails = [jnp.zeros((ROWS, QUART), F32), jnp.zeros((ROWS, QUART), F32)]
        for c in range(4):
            cols = slice(c * QUART, (c + 1) * QUART)
            y = _dot(h_ref[:, own], w_ref[own, cols]) + _dot(h_ref[:, side], w_ref[side, cols])
            y = y.astype(BF16)
            for i, ref in enumerate((oa_ref, ob_ref)):
                ref[:, at + c * QUART : at + (c + 1) * QUART] = y[i * ROWS : (i + 1) * ROWS]
                tail = y[2 * ROWS + i * TAIL : 2 * ROWS + (i + 1) * TAIL]
                tails[i] = tails[i] + _dot(_tail_row((ROWS, TAIL), 0, c), tail)
        for i, ref in enumerate((oa_ref, ob_ref)):
            ref[:, at + D : at + MSG] = tails[i].astype(BF16)
    _write_terms(pos_ref[0], pos_ref[1], h_ref, xt_ref, xg_ref, outs, turned, held, out_sems)


def _expert(pos, a, b, pieces):
    vmem = pl.BlockSpec(memory_space=pltpu.VMEM)
    return pl.pallas_call(
        _expert_kernel,
        in_specs=[pl.BlockSpec(memory_space=pltpu.SMEM)] + [vmem] * 2
        + [pl.BlockSpec(memory_space=pl.ANY)] * 8,
        out_specs=[vmem] * 2 + [pl.BlockSpec(memory_space=pltpu.HBM)] * 8,
        out_shape=[jax.ShapeDtypeStruct((ROWS, 2 * MSG), BF16)] * 2
        + [jax.ShapeDtypeStruct((4, 3 * HS, 128), BF16)] * 8,
        scratch_shapes=[
            pltpu.VMEM((SLOTS, 6 * HS), BF16),
            pltpu.VMEM((SLOTS, D), BF16),
            pltpu.VMEM((SLOTS, D), BF16),
            pltpu.VMEM((6 * HS, D), BF16),
            pltpu.VMEM((6 * HS, SLOTS), BF16),
            pltpu.VMEM((2, 16, 3 * HS, 128), BF16),
            pltpu.SemaphoreType.DMA((32,)),
            pltpu.SemaphoreType.DMA((32,)),
        ],
        compiler_params=pltpu.CompilerParams(vmem_limit_bytes=VMEM_LIMIT),
        cost_estimate=pl.CostEstimate(
            flops=36 * SLOTS * HS * D, bytes_accessed=16 * 2**20, transcendentals=2 * SLOTS * HS
        ),
        name="expert",
    )(pos, a, b, *pieces)


def _write_terms(y, x, h_ref, t_ref, g_ref, outs, turned, held, sems):
    for i in range(6):
        rows = slice(i * HS, (i + 1) * HS)
        turned[rows, :] = h_ref[:, rows].astype(F32).T.astype(BF16)
    copies = []
    for dy in range(4):
        cols = pl.ds(pl.multiple_of(lax.rem(y + dy, 4) * QUART, QUART), QUART)
        for half in range(2):
            base = half * 3 * HS
            gate_up = _dot(turned[base : base + 2 * HS, :], t_ref[:, cols]).astype(BF16)
            down = _dot(turned[base + 2 * HS : base + 3 * HS, :], g_ref[:, cols]).astype(BF16)
            for col in range(4):
                lanes = slice(col * 128, (col + 1) * 128)
                held[half, dy * 4 + col, : 2 * HS, :] = gate_up[:, lanes]
                held[half, dy * 4 + col, 2 * HS :, :] = down[:, lanes]
            for dx in range(4):
                out = outs[dx].at[dy] if half == 0 else outs[4 + dy].at[dx]
                copy = pltpu.make_async_copy(
                    held.at[half, dy * 4 + lax.rem(x + dx, 4)], out, sems.at[len(copies)]
                )
                copy.start()
                copies.append(copy)
    for copy in copies:
        copy.wait()


def _shift(x, axis, d):
    return lax.ppermute(x, axis, [(i, (i + d) % 4) for i in range(4)])


def _gather_near(piece, axis):
    got = {d: _shift(piece, axis, d) for d in (2, 1, 3)}
    return jnp.stack([piece, got[1], got[2], got[3]])


def _gather_far(stack, axis):
    got = {d: _shift(stack, axis, d) for d in (2, 1, 3)}
    return [stack, got[1], got[2], got[3]]


def _sum(parts):
    return sum(p.astype(F32) for p in parts)


def _scatter_terms(parts, first, second):
    half = _sum([parts[0]] + [_shift(parts[d], first, d) for d in (2, 1, 3)]).astype(BF16)
    return _sum([half[0]] + [_shift(half[d], second, d) for d in (2, 1, 3)])


def _exchange(x):
    return lax.all_to_all(
        x.reshape(8, FULL, 2 * MSG), "pair", split_axis=0, concat_axis=0, tiled=True
    ).reshape(ROWS, 2 * MSG)


def _add(a, b):
    return (a.astype(F32) + b.astype(F32)).astype(BF16)


def local(tokens, expert_ids, route_weight, cotangent, w_gate, w_up, w_down):
    ids = expert_ids.reshape(1, TOK)
    weight = route_weight.reshape(1, TOK)
    pos = jnp.stack([lax.axis_index("y"), lax.axis_index("x")]).astype(jnp.int32)
    own_piece = _pack(w_gate, w_up, w_down)
    side_piece = lax.ppermute(own_piece, "side", SWAP)
    sent = _send(ids, weight, tokens, cotangent)
    own_stack = _gather_near(own_piece, "y")
    sent, side_piece, own_stack = lax.optimization_barrier((sent, side_piece, own_stack))
    own_stack, side_stack = lax.optimization_barrier(
        (own_stack, _gather_near(side_piece, "x"))
    )
    pieces = _gather_far(own_stack, "x") + _gather_far(side_stack, "y")
    own, *pieces = lax.optimization_barrier((_exchange(sent), *pieces))
    from_core = lax.ppermute(own, "core", SWAP)
    out_own, out_core, *terms = _expert(pos, own, from_core, pieces)
    total = _add(out_own, lax.ppermute(out_core, "core", SWAP))
    own_terms = _scatter_terms(terms[:4], "x", "y")
    side_terms = _scatter_terms(terms[4:], "y", "x").astype(BF16)
    grads = (own_terms + lax.ppermute(side_terms, "side", SWAP).astype(F32)).astype(BF16)
    layer_out, token_grad = _take(ids, weight, _exchange(total))
    return layer_out, token_grad, grads[:HS], grads[HS : 2 * HS], grads[2 * HS :]


def solution(mesh):
    fine = Mesh(mesh.devices.reshape(4, 4, 8, 2, 2), ALL)
    return jax.shard_map(
        local,
        mesh=fine,
        in_specs=(P(ALL, None),) * 4 + (P(EXPERT, DP),) * 3,
        out_specs=(P(ALL, None),) * 2 + (P(EXPERT, DP),) * 3,
        check_vma=False,
    )
```
